32 devices in a mesh: frag: 2 (over x), occ: 2 (over core), vir: 8 (over z, y).
Axes of the slice: x: 2, y: 2, z: 4, core: 2. Of those that a mesh axis runs over, the one named last changes fastest.
Arguments:
- factors: bfloat16 [8, 1024, 3072], P(('frag', 'occ'), 'vir'), parts along dimension 0, may hold values from -2 to 2
- occ_energy: int32 [8], P('frag'), parts along dimension 0, may hold values from -1536 to -512
- vir_energy: int32 [2048], P('frag'), parts along dimension 0, may hold values from 512 to 4096
Outputs:
- density: float32 [8, 1024, 3072], P(('frag', 'occ'), 'vir'), parts along dimension 0
The draws below stay inside these ranges and needn't reach their ends.
There are 2 independent parts, one for each index of `frag`. The reference program is written for one: setup_inputs(seed, part) draws one part's arguments, and reference() takes and returns one part's arrays. A program takes and returns all parts, laid end to end along the dimension named above; each array names one. Nothing has to cross between parts.
Inputs may be any that keep to these rules, and one draw needn't show every extreme that they name: `occ_energy`: occupied energies lie at or below the highest occupied level -512. `vir_energy`: virtual energies lie at or above the lowest virtual level 512.
All inputs are finite; a program needn't handle non-finite values.
Results may differ from the reference program's by a relative error of at most 0.0055.
Values may be sent and summed in bfloat16 or wider, within the bound.
A program may use at most 128 MiB of HBM per device.

```python
import jax
import jax.numpy as jnp
from jax import lax

V = 1024
NAUX = 3072
OCC = 4


def place_ends(entries, key, smallest, high):
    index_at = [jax.random.randint(jax.random.fold_in(key, axis), (), 0, length) for axis, length in enumerate(entries.shape)]
    longest = entries.shape.index(max(entries.shape))
    next_to = index_at[:longest] + [(index_at[longest] + 1) % entries.shape[longest]] + index_at[longest + 1:]
    return entries.at[tuple(index_at)].set(smallest).at[tuple(next_to)].set(high)


def block_scale(stream_key, extent, cuts, low, high):
    loudness = 1.0
    for dim, shards_of in cuts:
        draws = jax.random.uniform(jax.random.fold_in(jax.random.fold_in(stream_key, 6), dim), (shards_of,), jnp.float32, low / len(cuts), high / len(cuts))
        loudness = loudness * jnp.repeat(jnp.exp(draws), extent[dim] // shards_of).reshape((-1,) + (1,) * (len(extent) - 1 - dim))
    return loudness


def noise(key, shape, deviation, most, cuts=(), kind=jnp.bfloat16):
    result = deviation * jax.random.normal(key, shape, jnp.float32)
    if cuts:
        result = result * block_scale(key, shape, cuts, -0.22, 0.18)
    return jnp.clip(result, -most, most).astype(kind)


def setup_inputs(seed: int = 0, part: int = 0) -> dict:
    arg_keys = jax.random.split(jax.random.key(seed), 4)
    part_keys = jax.random.split(jax.random.fold_in(arg_keys[3], part), 4)
    factors = noise(part_keys[0], (OCC, V, NAUX), 0.134, 2.0, ((0, 2), (1, 8)))
    occ_energy = place_ends(jax.random.randint(part_keys[1], (OCC,), -1536, -511), jax.random.fold_in(part_keys[1], 1), -1536, (-511) - 1).astype(jnp.int32)
    vir_energy = place_ends(jax.random.randint(part_keys[2], (V,), 512, 4097), jax.random.fold_in(part_keys[2], 1), 512, 4096).astype(jnp.int32)
    return dict(factors=factors, occ_energy=occ_energy, vir_energy=vir_energy)


energy_unit = 1.0 / 1024.0


def pair_density(factors, occ_energy, vir_energy, i):
    own = lax.dynamic_index_in_dim(factors, i, 0, keepdims=False)

    def step(j, acc):
        partner = lax.dynamic_index_in_dim(factors, j, 0, keepdims=False)
        direct = jnp.dot(own, partner.T, preferred_element_type=jnp.float32).astype(jnp.bfloat16)
        crossed = direct.T
        divisor = (occ_energy[i] + occ_energy[j] - vir_energy[:, None] - vir_energy[None, :]).astype(jnp.float32) * energy_unit
        amplitude = ((2.0 * direct.astype(jnp.float32) - crossed.astype(jnp.float32)) / divisor).astype(jnp.bfloat16)
        return acc + jnp.dot(amplitude, partner, preferred_element_type=jnp.float32)

    return lax.fori_loop(0, OCC, step, jnp.zeros((V, NAUX), jnp.float32))


def reference(factors, occ_energy, vir_energy):
    return lax.map(lambda i: pair_density(factors, occ_energy, vir_energy, i), jnp.arange(OCC, dtype=jnp.int32))
```

```python
import functools

import jax
import jax.numpy as jnp
from jax import lax
from jax.experimental import pallas as pl
from jax.experimental.pallas import tpu as pltpu
from jax.sharding import PartitionSpec as P

MESH = pl.DeviceIdType.MESH
energy_unit = 1.0 / 1024.0
NT = (((1,), (1,)), ((), ()))


def ring_is_natural(mesh):
    axis = list(mesh.axis_names).index("vir")
    devices = mesh.devices.swapaxes(axis, -1)
    line = devices.reshape(-1, devices.shape[-1])[0]
    coords = [getattr(d, "coords", None) for d in line]
    if any(c is None for c in coords):
        return False
    return all(
        sum(abs(p - q) for p, q in zip(a, b)) <= 1 for a, b in zip(coords, coords[1:])
    )


def grid_of(mesh):
    axis = list(mesh.axis_names).index("vir")
    devices = mesh.devices.swapaxes(axis, -1)
    line = devices.reshape(-1, devices.shape[-1])[0]
    coords = [getattr(d, "coords", None) for d in line]
    if len(line) != 8 or any(c is None for c in coords):
        return False

    def near(a, b):
        return sum(abs(p - q) for p, q in zip(coords[a], coords[b])) == 1

    return all(near(k, k + 1) for k in range(0, 8, 2)) and all(near(k, k + 2) for k in range(6))


def pair_amplitude(buf, a_slot, b_slot, base, own_occ, pair_occ, occ_local, vir_local, aux):
    wide = occ_local * vir_local
    here_own = buf[a_slot, 0:occ_local].reshape(wide, aux)
    here_all = buf[a_slot].reshape(2 * wide, aux)
    there_own = buf[b_slot, 0:occ_local].reshape(wide, aux)
    there_pair = buf[b_slot, occ_local:].reshape(wide, aux)
    with_own = lax.dot_general(
        here_all, there_own, NT, preferred_element_type=jnp.float32
    ).astype(jnp.bfloat16).astype(jnp.float32)
    with_pair = lax.dot_general(
        here_own, there_pair, NT, preferred_element_type=jnp.float32
    ).astype(jnp.bfloat16).astype(jnp.float32)

    def block(values, i, j):
        return values[i * vir_local:(i + 1) * vir_local, j * vir_local:(j + 1) * vir_local]

    bands = []
    for i in range(occ_local):
        band = []
        for j in range(occ_local):
            divisor = ((own_occ[i] + own_occ[j]) - base) * energy_unit
            band.append((2.0 * block(with_own, i, j) - block(with_own, j, i)) / divisor)
        for j in range(occ_local):
            divisor = ((own_occ[i] + pair_occ[j]) - base) * energy_unit
            crossed = block(with_own, occ_local + j, i)
            band.append((2.0 * block(with_pair, i, j) - crossed) / divisor)
        bands.append(jnp.concatenate(band, axis=1))
    return jnp.concatenate(bands, axis=0).astype(jnp.bfloat16)


E0, E1, M0, M1, F0, F1, G0, G1 = range(8)


def grid_kernel(chunks, x_ref, occ_ref, vir_ref, out_ref, buf, acc, sum_out, sum_in, local_sem,
                row_send, row_recv, end_send, end_recv, mid_send, mid_recv,
                pair_send, pair_recv, sum_send, sum_recv, out_sem):
    occ_local, vir_local, aux = x_ref.shape
    rows = vir_local // chunks
    core = lax.axis_index("occ")
    me = lax.axis_index("vir")
    pair = 1 - core
    column, row = me // 2, me % 2
    side = column // 2
    is_mid = (column + side) % 2
    mid, end = is_mid == 1, is_mid == 0

    def name_to_vir(slot):
        at, flip = slot // 2, slot % 2
        column_at = (1 - side) * at + side * (3 - at)
        return 2 * column_at + row + flip - 2 * row * flip

    other_row = 2 * column + 1 - row
    along = 2 * (is_mid * (3 * side) + (1 - is_mid) * (1 + side)) + row
    across = 2 * (3 - column) + row

    barrier = pltpu.get_barrier_semaphore()
    for target in ({"vir": other_row}, {"vir": along}, {"occ": pair}):
        pl.semaphore_signal(barrier, inc=1, device_id=target, device_id_type=MESH)

    @pl.when(mid)
    def _():
        pl.semaphore_signal(barrier, inc=1, device_id={"vir": across}, device_id_type=MESH)

    pl.semaphore_wait(barrier, 3 + is_mid)

    def part(slot, q):
        return buf.at[slot, pl.ds(0, occ_local), pl.ds(q * rows, rows)]

    def x_part(q):
        return x_ref.at[:, pl.ds(q * rows, rows)]

    def copy(src, dst, sends, recvs, order, q, target):
        return pltpu.make_async_remote_copy(
            src_ref=src, dst_ref=dst, send_sem=sends.at[order, q], recv_sem=recvs.at[order, q],
            device_id=target, device_id_type=MESH,
        )

    def to_row(order, slot, q, src=None):
        there = slot + 1 - 2 * (slot % 2)
        return copy(part(slot, q) if src is None else src, part(there, q),
                    row_send, row_recv, order, q, {"vir": other_row})

    def to_end(order, slot, q, src=None):
        return copy(part(slot, q) if src is None else src, part(slot, q),
                    end_send, end_recv, order, q, {"vir": along})

    def to_mid(order, slot, q, src=None):
        there = 6 - 2 * (slot // 2) + slot % 2
        return copy(part(slot, q) if src is None else src, part(there, q),
                    mid_send, mid_recv, order, q, {"vir": across})

    def to_pair(slot, q, src=None):
        there = buf.at[slot, pl.ds(occ_local, occ_local), pl.ds(q * rows, rows)]
        return copy(part(slot, q) if src is None else src, there,
                    pair_send, pair_recv, slot, q, {"occ": pair})

    def to_sum(i):
        return pltpu.make_async_remote_copy(
            src_ref=sum_out.at[i], dst_ref=sum_in.at[i], send_sem=sum_send.at[i],
            recv_sem=sum_recv.at[i], device_id={"vir": along}, device_id_type=MESH,
        )

    own = is_mid * M0 + (1 - is_mid) * E0
    own_copy = pltpu.make_async_copy(x_ref, buf.at[own, pl.ds(0, occ_local)], local_sem)

    @pl.loop(0, chunks)
    def _(q):
        @pl.when(end | (q == 0))
        def _():
            to_row(0, own, q, x_part(q)).start()

        to_end(0, own, q, x_part(q)).start()

        @pl.when(mid)
        def _():
            to_mid(0, own, q, x_part(q)).start()

    own_copy.start()

    @pl.loop(0, chunks)
    def _(q):
        to_pair(own, q, x_part(q)).start()

    acc[...] = jnp.zeros_like(acc)
    own_copy.wait()

    diagonal = lax.broadcasted_iota(jnp.int32, (vir_local, vir_local), 0) == (
        lax.broadcasted_iota(jnp.int32, (vir_local, vir_local), 1)
    )
    own_occ = [occ_ref[core * occ_local + i].astype(jnp.float32) for i in range(occ_local)]
    pair_occ = [occ_ref[pair * occ_local + i].astype(jnp.float32) for i in range(occ_local)]

    def energies(slot):
        return vir_ref[pl.ds(name_to_vir(slot), 1), :].astype(jnp.float32)

    step = 1024 if aux % 1024 == 0 else aux

    def compute(a_slot, b_slot, dest):
        a_column = jnp.sum(jnp.where(diagonal, energies(a_slot), 0.0), axis=1, keepdims=True)
        base = a_column + energies(b_slot)
        amplitude = pair_amplitude(
            buf, a_slot, b_slot, base, own_occ, pair_occ, occ_local, vir_local, aux
        )

        @pl.loop(0, aux // step)
        def _(t):
            columns = pl.ds(pl.multiple_of(t * step, step), step)
            there = buf[b_slot, :, :, columns].reshape(2 * occ_local * vir_local, step)
            piece = jnp.dot(amplitude, there, preferred_element_type=jnp.float32)
            acc[dest, :, :, columns] += piece.reshape(occ_local, vir_local, step)

    def arrivals(phase, q):
        @pl.when((phase == 1) & mid)
        def _():
            to_mid(0, M0, q).wait_recv()
            to_row(1, F0, q).start()

            @pl.when(q == chunks - 1)
            def _():
                @pl.loop(1, chunks)
                def _(later):
                    to_row(0, M0, later, x_part(later)).start()

            to_pair(F0, q).start()
            to_end(0, E0, q).wait_recv()
            to_mid(1, E0, q).start()
            to_pair(E0, q).start()

            @pl.when(q >= 2)
            def _():
                to_row(1, F0, q - 2).wait_recv()
                to_pair(F1, q - 2).start()

        @pl.when((phase == 1) & end)
        def _():
            to_end(0, M0, q).wait_recv()
            to_row(1, M0, q).start()
            to_pair(M0, q).start()
            to_row(0, E0, q).wait_recv()
            to_end(1, E1, q).start()
            to_pair(E1, q).start()

        @pl.when((phase == 2) & mid)
        def _():
            to_mid(1, E0, q).wait_recv()
            to_end(1, G0, q).start()

            @pl.when(q == 0)
            def _():
                for late in (chunks - 2, chunks - 1):
                    to_row(1, F0, late).wait_recv()
                    to_pair(F1, late).start()

            @pl.when(q == chunks - 1)
            def _():
                for i in range(occ_local):
                    to_sum(i).start()

            to_row(2, G0, q).start()
            to_pair(G0, q).start()
            to_end(1, E1, q).wait_recv()
            to_pair(E1, q).start()
            to_row(0, M0, q).wait_recv()
            to_pair(M1, q).start()

        @pl.when((phase == 2) & end)
        def _():
            to_end(1, G0, q).wait_recv()
            to_row(2, G0, q).start()
            to_pair(G0, q).start()
            to_row(1, M0, q).wait_recv()
            to_pair(M1, q).start()

        @pl.when(phase == 3)
        def _():
            to_row(2, G0, q).wait_recv()
            to_pair(G1, q).start()

    none = 10**chunks - 10
    mid_code = {1: none + M0, 2: none + 5454 - 99990 + 0, 3: none + 613 - 990, 4: none + G1}
    end_code = {1: none + E0, 2: none + 12 - 90, 3: none + 63 - 90, 4: none + G1}

    def by_phase(phase, code):
        return jnp.where(phase == 1, code[1], jnp.where(phase == 2, code[2], jnp.where(phase == 3, code[3], code[4])))

    def phase_body(phase, carry):
        blocks = is_mid * by_phase(phase, mid_code) + (1 - is_mid) * by_phase(phase, end_code)
        count = jnp.where(phase == 4, 1, chunks)

        @pl.loop(0, count)
        def _(q):
            arrivals(phase, q)
            scale = 1
            for power in range(1, chunks):
                scale = jnp.where(q == power, 10**power, scale)
            b_slot = (blocks // scale) % 10
            sums = mid & (phase == 2)

            @pl.when(sums & (q == 2))
            def _():
                for i in range(occ_local):
                    sum_out[i] = acc[1, i].astype(jnp.bfloat16)

            @pl.when(b_slot < 8)
            def _():
                @pl.when(jnp.logical_not(sums & (q >= 2)))
                def _():
                    @pl.loop(0, chunks)
                    def _(part_q):
                        to_pair(b_slot, part_q).wait_recv()

                @pl.when(sums & (q == 0))
                def _():
                    @pl.loop(0, chunks)
                    def _(part_q):
                        to_pair(E0, part_q).wait_recv()

                for_end = jnp.where(sums & (q < 2), 1, 0)
                compute((1 - for_end) * own, b_slot, for_end)

        return carry

    lax.fori_loop(1, 5, phase_body, 0)

    def write_out(i):
        return pltpu.make_async_copy(acc.at[0, i], out_ref.at[i], out_sem.at[i])

    for i in range(occ_local):
        @pl.when(end)
        def _():
            to_sum(i).wait_recv()
            acc[0, i] += sum_in[i].astype(jnp.float32)

        write_out(i).start()

    @pl.loop(0, chunks)
    def _(q):
        to_row(0, own, q, x_part(q)).wait_send()
        to_end(0, own, q, x_part(q)).wait_send()
        to_row(2, G0, q).wait_send()
        for slot in range(8):
            @pl.when((slot != F0) & (slot != F1) | mid)
            def _():
                to_pair(slot, q).wait_send()

        @pl.when(mid)
        def _():
            to_mid(0, own, q, x_part(q)).wait_send()
            to_mid(1, E0, q).wait_send()
            to_row(1, F0, q).wait_send()
            to_end(1, G0, q).wait_send()

        @pl.when(end)
        def _():
            to_row(1, M0, q).wait_send()
            to_end(1, E1, q).wait_send()

    @pl.when(mid)
    def _():
        for i in range(occ_local):
            to_sum(i).wait_send()

    for i in range(occ_local):
        write_out(i).wait()


def kernel(n, natural, chunks, x_ref, occ_ref, vir_ref, out_ref, buf, local_sem,
           right_send, right_recv, left_send, left_recv, pair_send, pair_recv):
    occ_local, vir_local, aux = x_ref.shape
    half = n // 2
    rows = vir_local // chunks
    core = lax.axis_index("occ")
    me = lax.axis_index("vir")

    if natural:
        place = me

        def at_place(k):
            return k
    else:
        odd = me % 2
        place = (1 - odd) * (me // 2) + odd * (n - 1 - me // 2)

        def at_place(k):
            down = k // half
            return (1 - down) * (2 * k) + down * (2 * (n - k) - 1)

    right = at_place((place + 1) % n)
    left = at_place((place + n - 1) % n)
    pair = 1 - core

    barrier = pltpu.get_barrier_semaphore()
    for target in ({"vir": right}, {"vir": left}, {"occ": pair}):
        pl.semaphore_signal(barrier, inc=1, device_id=target, device_id_type=MESH)
    pl.semaphore_wait(barrier, 3)

    def own_part(slot, q):
        return buf.at[slot, pl.ds(0, occ_local), pl.ds(q * rows, rows)]

    def pair_part(slot, q):
        return buf.at[slot, pl.ds(occ_local, occ_local), pl.ds(q * rows, rows)]

    def to_right(slot, q, src=None):
        return pltpu.make_async_remote_copy(
            src_ref=own_part(slot, q) if src is None else src,
            dst_ref=own_part(slot + 1, q),
            send_sem=right_send.at[slot, q],
            recv_sem=right_recv.at[slot + 1, q],
            device_id={"vir": right},
            device_id_type=MESH,
        )

    def to_left(slot, q, src=None):
        return pltpu.make_async_remote_copy(
            src_ref=own_part(slot % n, q) if src is None else src,
            dst_ref=own_part(slot - 1, q),
            send_sem=left_send.at[n - slot, q],
            recv_sem=left_recv.at[n - slot + 1, q],
            device_id={"vir": left},
            device_id_type=MESH,
        )

    def to_pair(slot, q, src=None):
        return pltpu.make_async_remote_copy(
            src_ref=own_part(slot, q) if src is None else src,
            dst_ref=pair_part(slot, q),
            send_sem=pair_send.at[slot, q],
            recv_sem=pair_recv.at[slot, q],
            device_id={"occ": pair},
            device_id_type=MESH,
        )

    def x_part(q):
        return x_ref.at[:, pl.ds(q * rows, rows)]

    own_copy = pltpu.make_async_copy(x_ref, buf.at[0, pl.ds(0, occ_local)], local_sem)
    for q in range(chunks):
        to_right(0, q, x_part(q)).start()
        to_left(n, chunks - 1 - q, x_part(chunks - 1 - q)).start()
    own_copy.start()
    for q in range(chunks):
        to_pair(0, q, x_part(q)).start()
    out_ref[...] = jnp.zeros_like(out_ref)
    own_copy.wait()

    diagonal = lax.broadcasted_iota(jnp.int32, (vir_local, vir_local), 0) == (
        lax.broadcasted_iota(jnp.int32, (vir_local, vir_local), 1)
    )
    own_row = vir_ref[pl.ds(me, 1), :].astype(jnp.float32)
    own_column = jnp.sum(jnp.where(diagonal, own_row, 0.0), axis=1, keepdims=True)
    own_occ = [occ_ref[core * occ_local + i].astype(jnp.float32) for i in range(occ_local)]
    pair_occ = [occ_ref[pair * occ_local + i].astype(jnp.float32) for i in range(occ_local)]

    def compute(slot):
        source = at_place((place - slot + n) % n)
        energy_row = vir_ref[pl.ds(source, 1), :].astype(jnp.float32)
        base = own_column + energy_row
        amplitude = pair_amplitude(
            buf, 0, slot, base, own_occ, pair_occ, occ_local, vir_local, aux
        )

        step = 1024 if aux % 1024 == 0 else aux

        @pl.loop(0, aux // step)
        def _(t):
            columns = pl.ds(pl.multiple_of(t * step, step), step)
            there = buf[slot, :, :, columns].reshape(2 * occ_local * vir_local, step)
            part = jnp.dot(amplitude, there, preferred_element_type=jnp.float32)
            out_ref[:, :, columns] += part.reshape(occ_local, vir_local, step)

    def step_body(h, carry):
        @pl.when(h == 0)
        def _():
            for q in range(chunks):
                to_pair(0, q).wait_recv()

        @pl.when((h > 0) & (h < half))
        def _():
            for q in range(chunks):
                back = chunks - 1 - q
                to_right(h - 1, q).wait_recv()
                if q < chunks // 2:
                    to_right(h, q).start()
                else:
                    @pl.when(h < half - 1)
                    def _():
                        to_right(h, q).start()
                to_pair(h, q).start()
                to_left(n - h + 1, back).wait_recv()
                if back >= chunks // 2:
                    to_left(n - h, back).start()
                else:
                    @pl.when(h < half - 1)
                    def _():
                        to_left(n - h, back).start()
                to_pair(n - h, back).start()
            for q in range(chunks):
                to_pair(h, q).wait_recv()
                to_pair(n - h, chunks - 1 - q).wait_recv()

        @pl.when(h == half)
        def _():
            for q in range(chunks // 2):
                back = chunks - 1 - q
                to_right(half - 1, q).wait_recv()
                to_pair(half, q).start()
                to_left(half + 1, back).wait_recv()
                to_pair(half, back).start()
            for q in range(chunks):
                to_pair(half, q).wait_recv()

        both = jnp.where((h > 0) & (h < half), 2, 1)

        @pl.loop(0, both)
        def _(side):
            compute(h * (1 - side) + (n - h) * side)

        return carry

    lax.fori_loop(0, half + 1, step_body, 0)

    for h in range(half):
        for q in range(chunks):
            if h < half - 1 or q < chunks // 2:
                to_right(h, q).wait_send()
            if h < half - 1 or q >= chunks // 2:
                to_left(n - h, q, x_part(q) if h == 0 else None).wait_send()
    for slot in range(n):
        for q in range(chunks):
            to_pair(slot, q).wait_send()


def solution(mesh):
    n = mesh.shape["vir"]
    natural = ring_is_natural(mesh)
    grid = grid_of(mesh)

    def on_device(factors, occ_energy, vir_energy):
        occ_local, vir_local, aux = factors.shape
        dma = pltpu.SemaphoreType.DMA
        blocks = pltpu.VMEM((n, 2 * occ_local, vir_local, aux), jnp.bfloat16)
        if grid:
            chunks = 8
            body = functools.partial(grid_kernel, chunks)
            scratch = [
                blocks,
                pltpu.VMEM((2, occ_local, vir_local, aux), jnp.float32),
                pltpu.VMEM((occ_local, vir_local, aux), jnp.bfloat16),
                pltpu.VMEM((occ_local, vir_local, aux), jnp.bfloat16),
                dma,
                *[dma((3, chunks))] * 2,
                *[dma((2, chunks))] * 4,
                *[dma((n, chunks))] * 2,
                *[dma((occ_local,))] * 3,
            ]
        else:
            chunks = 4
            body = functools.partial(kernel, n, natural, chunks)
            scratch = [
                blocks,
                dma,
                *[dma((n // 2, chunks)), dma((n // 2 + 1, chunks))] * 2,
                *[dma((n, chunks))] * 2,
            ]
        return pl.pallas_call(
            body,
            out_shape=pltpu.VMEM((occ_local, vir_local, aux), jnp.float32),
            in_specs=[
                pl.BlockSpec(memory_space=pl.ANY),
                pl.BlockSpec(memory_space=pltpu.SMEM),
                pl.BlockSpec(memory_space=pltpu.VMEM),
            ],
            out_specs=pl.BlockSpec(memory_space=pl.ANY if grid else pltpu.VMEM),
            scratch_shapes=scratch,
            compiler_params=pltpu.CompilerParams(
                collective_id=0, has_side_effects=True, vmem_limit_bytes=56 * 1024 * 1024
            ),
            name="ring_density",
        )(pltpu.with_memory_space_constraint(factors, pltpu.HBM), occ_energy, vir_energy.reshape(n, vir_local))

    return jax.shard_map(
        on_device,
        mesh=mesh,
        in_specs=(P(("frag", "occ"), "vir", None), P("frag"), P("frag")),
        out_specs=P(("frag", "occ"), "vir", None),
        check_vma=False,
    )
```

```python
import functools

import jax
import jax.numpy as jnp
from jax import lax
from jax.experimental import pallas as pl
from jax.experimental.pallas import tpu as pltpu
from jax.sharding import PartitionSpec as P

MESH = pl.DeviceIdType.MESH
energy_unit = 1.0 / 1024.0
NT = (((1,), (1,)), ((), ()))


def ring_is_natural(mesh):
    axis = list(mesh.axis_names).index("vir")
    devices = mesh.devices.swapaxes(axis, -1)
    line = devices.reshape(-1, devices.shape[-1])[0]
    coords = [getattr(d, "coords", None) for d in line]
    if any(c is None for c in coords):
        return False
    return all(
        sum(abs(p - q) for p, q in zip(a, b)) <= 1 for a, b in zip(coords, coords[1:])
    )


def grid_of(mesh):
    axis = list(mesh.axis_names).index("vir")
    devices = mesh.devices.swapaxes(axis, -1)
    line = devices.reshape(-1, devices.shape[-1])[0]
    coords = [getattr(d, "coords", None) for d in line]
    if len(line) != 8 or any(c is None for c in coords):
        return False

    def near(a, b):
        return sum(abs(p - q) for p, q in zip(coords[a], coords[b])) == 1

    return all(near(k, k + 1) for k in range(0, 8, 2)) and all(near(k, k + 2) for k in range(6))


def pair_amplitude(buf, a_slot, b_slot, base, own_occ, pair_occ, occ_local, vir_local, aux):
    wide = occ_local * vir_local
    here_own = buf[a_slot, 0:occ_local].reshape(wide, aux)
    here_all = buf[a_slot].reshape(2 * wide, aux)
    there_own = buf[b_slot, 0:occ_local].reshape(wide, aux)
    there_pair = buf[b_slot, occ_local:].reshape(wide, aux)
    with_own = lax.dot_general(
        here_all, there_own, NT, preferred_element_type=jnp.float32
    ).astype(jnp.bfloat16).astype(jnp.float32)
    with_pair = lax.dot_general(
        here_own, there_pair, NT, preferred_element_type=jnp.float32
    ).astype(jnp.bfloat16).astype(jnp.float32)

    def block(values, i, j):
        return values[i * vir_local:(i + 1) * vir_local, j * vir_local:(j + 1) * vir_local]

    bands = []
    for i in range(occ_local):
        band = []
        for j in range(occ_local):
            divisor = ((own_occ[i] + own_occ[j]) - base) * energy_unit
            band.append((2.0 * block(with_own, i, j) - block(with_own, j, i)) / divisor)
        for j in range(occ_local):
            divisor = ((own_occ[i] + pair_occ[j]) - base) * energy_unit
            crossed = block(with_own, occ_local + j, i)
            band.append((2.0 * block(with_pair, i, j) - crossed) / divisor)
        bands.append(jnp.concatenate(band, axis=1))
    return jnp.concatenate(bands, axis=0).astype(jnp.bfloat16)


E0, E1, M0, M1, F0, F1, G0, G1 = range(8)


def pick(s, table, default=-1):
    value = default
    for step, entry in table.items():
        value = jnp.where(s == step, entry, value)
    return value


def grid_kernel(share, x_ref, occ_ref, vir_ref, out_ref, buf, sum_acc, sum_out, sum_in, amp,
                local_sem, row_send, row_recv, end_send, end_recv, mid_send, mid_recv,
                pair_send, pair_recv, sum_send, sum_recv, amp_send, amp_recv):
    occ_local, vir_local, aux = x_ref.shape
    parts = row_send.shape[1] // occ_local
    rows = vir_local // parts
    chunks = parts * occ_local
    tiles = sum_send.shape[0]
    step = aux // tiles
    early = tiles // 2
    cut = early * step
    core = lax.axis_index("occ")
    me = lax.axis_index("vir")
    pair = 1 - core
    column, row = me // 2, me % 2
    side = column // 2
    is_mid = (column + side) % 2
    mid, end = is_mid == 1, is_mid == 0

    def name_to_vir(slot):
        at, flip = slot // 2, slot % 2
        column_at = (1 - side) * at + side * (3 - at)
        return 2 * column_at + row + flip - 2 * row * flip

    other_row = 2 * column + 1 - row
    along = 2 * (is_mid * (3 * side) + (1 - is_mid) * (1 + side)) + row
    across = 2 * (3 - column) + row

    barrier = pltpu.get_barrier_semaphore()
    for target in ({"vir": other_row}, {"vir": along}, {"occ": pair}):
        pl.semaphore_signal(barrier, inc=1, device_id=target, device_id_type=MESH)

    @pl.when(mid)
    def _():
        pl.semaphore_signal(barrier, inc=1, device_id={"vir": across}, device_id_type=MESH)

    pl.semaphore_wait(barrier, 3 + is_mid)

    def part(slot, c, few=False):
        where = (slot, c % occ_local, pl.ds((c // occ_local) * rows, rows))
        return buf.at[where + ((pl.ds(0, cut),) if few else ())]

    def x_part(c):
        return x_ref.at[c % occ_local, pl.ds((c // occ_local) * rows, rows)]

    def copy(src, dst, sends, recvs, order, c, target):
        return pltpu.make_async_remote_copy(
            src_ref=src, dst_ref=dst, send_sem=sends.at[order, c], recv_sem=recvs.at[order, c],
            device_id=target, device_id_type=MESH,
        )

    def to_row(order, slot, c, src=None, few=False):
        there = slot + 1 - 2 * (slot % 2)
        return copy(part(slot, c, few) if src is None else src, part(there, c, few),
                    row_send, row_recv, order, c, {"vir": other_row})

    def to_end(order, slot, c, src=None, few=False):
        return copy(part(slot, c, few) if src is None else src, part(slot, c, few),
                    end_send, end_recv, order, c, {"vir": along})

    def to_mid(order, slot, c, src=None):
        there = 6 - 2 * (slot // 2) + slot % 2
        return copy(part(slot, c) if src is None else src, part(there, c),
                    mid_send, mid_recv, order, c, {"vir": across})

    def to_pair(slot, q, few=False):
        tail = (pl.ds(q * rows, rows),) + ((pl.ds(0, cut),) if few else ())
        return copy(buf.at[(slot, pl.ds(0, occ_local)) + tail],
                    buf.at[(slot, pl.ds(occ_local, occ_local)) + tail],
                    pair_send, pair_recv, slot, q, {"occ": pair})

    def to_sum(t, i):
        where = (i, pl.ds(0, vir_local), pl.ds(t * step, step))
        return copy(sum_out.at[where], sum_in.at[where], sum_send, sum_recv, t, i, {"vir": along})

    def to_amp(k):
        return pltpu.make_async_remote_copy(
            src_ref=amp.at[k], dst_ref=amp.at[k], send_sem=amp_send.at[k], recv_sem=amp_recv.at[k],
            device_id={"vir": along}, device_id_type=MESH,
        )

    own = is_mid * M0 + (1 - is_mid) * E0
    own_copy = pltpu.make_async_copy(x_ref, buf.at[own, pl.ds(0, occ_local)], local_sem)

    @pl.when(mid)
    def _():
        to_mid(1, M0, 0, x_part(0)).start()

    @pl.loop(0, chunks)
    def _(c):
        @pl.when(end)
        def _():
            to_end(0, E0, c, x_part(c)).start()

        to_row(0, own, c, x_part(c)).start()

    own_copy.start()
    out_ref[...] = jnp.zeros_like(out_ref)

    @pl.when(mid)
    def _():
        sum_acc[...] = jnp.zeros_like(sum_acc)

    own_copy.wait()

    @pl.loop(0, parts)
    def _(q):
        to_pair(own, q).start()

    diagonal = lax.broadcasted_iota(jnp.int32, (vir_local, vir_local), 0) == (
        lax.broadcasted_iota(jnp.int32, (vir_local, vir_local), 1)
    )
    own_occ = [occ_ref[core * occ_local + i].astype(jnp.float32) for i in range(occ_local)]
    pair_occ = [occ_ref[pair * occ_local + i].astype(jnp.float32) for i in range(occ_local)]

    def energies(slot):
        return vir_ref[pl.ds(name_to_vir(slot), 1), :].astype(jnp.float32)

    def amplitude(a_slot, b_slot):
        a_column = jnp.sum(jnp.where(diagonal, energies(a_slot), 0.0), axis=1, keepdims=True)
        base = a_column + energies(b_slot)
        return pair_amplitude(
            buf, a_slot, b_slot, base, own_occ, pair_occ, occ_local, vir_local, aux
        )

    def product(k, b_slot, t):
        columns = pl.ds(pl.multiple_of(t * step, step), step)
        there = buf[b_slot, :, :, columns].reshape(2 * occ_local * vir_local, step)
        piece = jnp.dot(amp[k], there, preferred_element_type=jnp.float32)
        return columns, piece.reshape(occ_local, vir_local, step)

    def arrive(role, s, first, count, body, order=None):
        @pl.when(role & (s >= first) & (s < first + count))
        def _():
            c = s - first
            body(c if order is None else order(c))

    def pair_on(slot, c, last=occ_local - 1, few=False):
        @pl.when(c % occ_local == last)
        def _():
            to_pair(slot, c // occ_local, few).start()

    turn = chunks + 2
    close = 2 * chunks + 1

    def mid_arrivals(s):
        def e0(c):
            to_end(0, E0, c).wait_recv()
            to_mid(0, E0, c).start()
            pair_on(E0, c)

        def f0_first(c):
            to_mid(1, M0, 0).wait_recv()
            to_end(1, F0, 0, few=True).start()
            to_row(1, F0, 0).start()

        def g0(c):
            to_mid(0, E0, c).wait_recv()
            to_end(0, G0, c).start()
            pair_on(G0, c)

        def m1(c):
            to_row(0, M0, c).wait_recv()
            pair_on(M1, c)

        def own_rest(_):
            @pl.loop(1, chunks)
            def _(c):
                to_mid(1, M0, c, x_part(c)).start()

        def f0(c):
            to_mid(1, M0, c).wait_recv()
            to_end(1, F0, c, few=True).start()
            to_row(1, F0, c).start()
            pair_on(F0, c)

        def f1(c):
            to_row(1, F0, c).wait_recv()
            pair_on(F1, c)

        def g0_row(_):
            @pl.loop(0, chunks - share)
            def _(c):
                to_row(2, G0, c).start()

        def e1(c):
            to_end(1, E1, c).wait_recv()

            @pl.when(c >= chunks - share)
            def _():
                to_mid(2, E1, c).start()

            pair_on(E1, c, 0)

        def g1(c):
            to_row(2, G0, c).wait_recv()
            pair_on(G1, c)

        def g1_rest(_):
            @pl.loop(chunks - share, chunks)
            def _(c):
                to_mid(2, E1, c).wait_recv()
                pair_on(G1, c)

        arrive(mid, s, 0, chunks, e0)
        arrive(mid, s, chunks - 1, 1, own_rest)
        arrive(mid, s, 1, 1, f0_first)
        arrive(mid, s, 2, chunks, g0)
        arrive(mid, s, 1, chunks, m1)
        arrive(mid, s, turn, chunks - 1, f0, lambda c: c + 1)
        arrive(mid, s, turn + 2, chunks, f1)
        arrive(mid, s, close, 1, g0_row)
        arrive(mid, s, turn + 4, chunks, e1, lambda c: chunks - 1 - c)
        arrive(mid, s, close + 3, chunks - share, g1)
        arrive(mid, s, close + 3 + chunks - share, 1, g1_rest)

    def end_arrivals(s):
        def e1(c):
            to_row(0, E0, c).wait_recv()
            pair_on(E1, c)

        def f0_first(c):
            to_end(1, F0, 0, few=True).wait_recv()
            to_row(2, F0, 0, few=True).start()

        def g0(c):
            to_end(0, G0, c).wait_recv()
            to_row(1, G0, c).start()
            pair_on(G0, c)

        def e1_along(_):
            @pl.loop(0, chunks)
            def _(c):
                to_end(1, E1, chunks - 1 - c).start()

        def f0(c):
            to_end(1, F0, c, few=True).wait_recv()
            to_row(2, F0, c, few=True).start()
            pair_on(F0, c, few=True)

        def g1(c):
            to_row(1, G0, c).wait_recv()
            pair_on(G1, c)

        def f1(c):
            to_row(2, F0, c, few=True).wait_recv()
            pair_on(F1, c, few=True)

        arrive(end, s, 1, chunks, e1)
        arrive(end, s, 3, 1, f0_first)
        arrive(end, s, 4, chunks, g0)
        arrive(end, s, turn + 1, 1, e1_along)
        arrive(end, s, turn + 3, chunks - 1, f0, lambda c: c + 1)
        arrive(end, s, turn + 1, chunks, g1)
        arrive(end, s, turn + 9, chunks, f1)

    last = close + 4 + chunks - share
    mid_for_end = {turn: M0, turn + 1: M1, close: F0, close + 3: F1}
    mid_own = {turn + 3: M0, turn + 5: E0, turn + 7: M1, turn + 9: G0, close + 4: F0,
               close + 5: F1, close + 6: E1, last: G1}
    end_own = {2: E0, turn: E1, turn + 3: G0, close + 3: G1}
    end_given = {close + 7: F0, close + 10: F1}
    steps = max(last, close + 10) + 1

    def one(s, carry):
        mid_arrivals(s)
        end_arrivals(s)
        for_end = is_mid * (pick(s, mid_for_end) + 1) - 1
        for_own = is_mid * pick(s, mid_own) + (1 - is_mid) * pick(s, end_own)
        given = (1 - is_mid) * (pick(s, end_given) + 1) - 1
        far = (for_end == F0) | (for_end == F1)
        b_slot = jnp.maximum(jnp.maximum(for_end, for_own), given)
        k = jnp.where(far | (given >= 0), 1 + b_slot % 2, 0)

        new = end | (for_end >= 0) | (b_slot == G0) | (b_slot == E1) | (b_slot == G1)

        @pl.when((b_slot >= 0) & (given < 0) & new)
        def _():
            @pl.loop(0, parts)
            def _(q):
                to_pair(b_slot, q).wait_recv()

        @pl.when(mid & (s == turn))
        def _():
            @pl.loop(0, parts)
            def _(q):
                to_pair(E0, q).wait_recv()

        @pl.when((for_end >= 0) | (for_own >= 0))
        def _():
            a_slot = jnp.where(for_end >= 0, E0, own)
            amp[k] = amplitude(a_slot, b_slot)

        @pl.when(far)
        def _():
            to_amp(k).start()

        @pl.when(given >= 0)
        def _():
            to_amp(k).wait_recv()

            @pl.loop(0, parts)
            def _(q):
                to_pair(b_slot, q, few=True).wait_recv()

        @pl.when((for_own >= 0) | (given >= 0))
        def _():
            @pl.loop(0, jnp.where(given >= 0, early, tiles))
            def _(t):
                columns, piece = product(k, b_slot, t)
                out_ref[:, :, columns] += piece

        @pl.when(for_end >= 0)
        def _():
            @pl.loop(jnp.where(far, early, 0), tiles)
            def _(t):
                columns, piece = product(k, b_slot, t)
                sum_acc[:, :, columns] += piece

        @pl.when((for_end == M1) | (for_end == F1))
        def _():
            low = jnp.where(far, early, 0)

            @pl.loop(low, low + early)
            def _(t):
                columns = pl.ds(pl.multiple_of(t * step, step), step)
                for i in range(occ_local):
                    sum_out[i, :, columns] = sum_acc[i, :, columns].astype(jnp.bfloat16)
                    to_sum(t, i).start()

        return carry

    lax.fori_loop(0, steps, one, 0)

    @pl.when(end)
    def _():
        @pl.loop(0, tiles)
        def _(t):
            columns = pl.ds(pl.multiple_of(t * step, step), step)
            for i in range(occ_local):
                to_sum(t, i).wait_recv()
                out_ref[i, :, columns] += sum_in[i, :, columns].astype(jnp.float32)

    @pl.loop(0, chunks)
    def _(c):
        to_row(0, own, c, x_part(c)).wait_send()
        to_row(1, F0, c).wait_send()
        to_end(0, E0, c).wait_send()

        @pl.when(mid)
        def _():
            to_end(1, F0, c, few=True).wait_send()
            to_mid(0, E0, c).wait_send()
            to_mid(1, M0, c, x_part(c)).wait_send()

            @pl.when(c < chunks - share)
            def _():
                to_row(2, G0, c).wait_send()

            @pl.when(c >= chunks - share)
            def _():
                to_mid(2, E1, c).wait_send()

        @pl.when(end)
        def _():
            to_end(1, E1, c).wait_send()
            to_row(2, F0, c, few=True).wait_send()

    @pl.loop(0, parts)
    def _(q):
        for slot in (E0, E1, G0, G1):
            to_pair(slot, q).wait_send()

        for slot in (M0, M1):
            @pl.when(mid)
            def _():
                to_pair(slot, q).wait_send()

        for slot in (F0, F1):
            @pl.when(mid)
            def _():
                to_pair(slot, q).wait_send()

            @pl.when(end)
            def _():
                to_pair(slot, q, few=True).wait_send()

    @pl.when(mid)
    def _():
        for k in (1, 2):
            to_amp(k).wait_send()
        for t in range(tiles):
            for i in range(occ_local):
                to_sum(t, i).wait_send()


def kernel(n, natural, chunks, x_ref, occ_ref, vir_ref, out_ref, buf, local_sem,
           right_send, right_recv, left_send, left_recv, pair_send, pair_recv):
    occ_local, vir_local, aux = x_ref.shape
    half = n // 2
    rows = vir_local // chunks
    core = lax.axis_index("occ")
    me = lax.axis_index("vir")

    if natural:
        place = me

        def at_place(k):
            return k
    else:
        odd = me % 2
        place = (1 - odd) * (me // 2) + odd * (n - 1 - me // 2)

        def at_place(k):
            down = k // half
            return (1 - down) * (2 * k) + down * (2 * (n - k) - 1)

    right = at_place((place + 1) % n)
    left = at_place((place + n - 1) % n)
    pair = 1 - core

    barrier = pltpu.get_barrier_semaphore()
    for target in ({"vir": right}, {"vir": left}, {"occ": pair}):
        pl.semaphore_signal(barrier, inc=1, device_id=target, device_id_type=MESH)
    pl.semaphore_wait(barrier, 3)

    def own_part(slot, q):
        return buf.at[slot, pl.ds(0, occ_local), pl.ds(q * rows, rows)]

    def pair_part(slot, q):
        return buf.at[slot, pl.ds(occ_local, occ_local), pl.ds(q * rows, rows)]

    def to_right(slot, q, src=None):
        return pltpu.make_async_remote_copy(
            src_ref=own_part(slot, q) if src is None else src,
            dst_ref=own_part(slot + 1, q),
            send_sem=right_send.at[slot, q],
            recv_sem=right_recv.at[slot + 1, q],
            device_id={"vir": right},
            device_id_type=MESH,
        )

    def to_left(slot, q, src=None):
        return pltpu.make_async_remote_copy(
            src_ref=own_part(slot % n, q) if src is None else src,
            dst_ref=own_part(slot - 1, q),
            send_sem=left_send.at[n - slot, q],
            recv_sem=left_recv.at[n - slot + 1, q],
            device_id={"vir": left},
            device_id_type=MESH,
        )

    def to_pair(slot, q, src=None):
        return pltpu.make_async_remote_copy(
            src_ref=own_part(slot, q) if src is None else src,
            dst_ref=pair_part(slot, q),
            send_sem=pair_send.at[slot, q],
            recv_sem=pair_recv.at[slot, q],
            device_id={"occ": pair},
            device_id_type=MESH,
        )

    def x_part(q):
        return x_ref.at[:, pl.ds(q * rows, rows)]

    own_copy = pltpu.make_async_copy(x_ref, buf.at[0, pl.ds(0, occ_local)], local_sem)
    for q in range(chunks):
        to_right(0, q, x_part(q)).start()
        to_left(n, chunks - 1 - q, x_part(chunks - 1 - q)).start()
    own_copy.start()
    for q in range(chunks):
        to_pair(0, q, x_part(q)).start()
    out_ref[...] = jnp.zeros_like(out_ref)
    own_copy.wait()

    diagonal = lax.broadcasted_iota(jnp.int32, (vir_local, vir_local), 0) == (
        lax.broadcasted_iota(jnp.int32, (vir_local, vir_local), 1)
    )
    own_row = vir_ref[pl.ds(me, 1), :].astype(jnp.float32)
    own_column = jnp.sum(jnp.where(diagonal, own_row, 0.0), axis=1, keepdims=True)
    own_occ = [occ_ref[core * occ_local + i].astype(jnp.float32) for i in range(occ_local)]
    pair_occ = [occ_ref[pair * occ_local + i].astype(jnp.float32) for i in range(occ_local)]

    def compute(slot):
        source = at_place((place - slot + n) % n)
        energy_row = vir_ref[pl.ds(source, 1), :].astype(jnp.float32)
        base = own_column + energy_row
        amplitude = pair_amplitude(
            buf, 0, slot, base, own_occ, pair_occ, occ_local, vir_local, aux
        )

        step = 1024 if aux % 1024 == 0 else aux

        @pl.loop(0, aux // step)
        def _(t):
            columns = pl.ds(pl.multiple_of(t * step, step), step)
            there = buf[slot, :, :, columns].reshape(2 * occ_local * vir_local, step)
            part = jnp.dot(amplitude, there, preferred_element_type=jnp.float32)
            out_ref[:, :, columns] += part.reshape(occ_local, vir_local, step)

    def step_body(h, carry):
        @pl.when(h == 0)
        def _():
            for q in range(chunks):
                to_pair(0, q).wait_recv()

        @pl.when((h > 0) & (h < half))
        def _():
            for q in range(chunks):
                back = chunks - 1 - q
                to_right(h - 1, q).wait_recv()
                if q < chunks // 2:
                    to_right(h, q).start()
                else:
                    @pl.when(h < half - 1)
                    def _():
                        to_right(h, q).start()
                to_pair(h, q).start()
                to_left(n - h + 1, back).wait_recv()
                if back >= chunks // 2:
                    to_left(n - h, back).start()
                else:
                    @pl.when(h < half - 1)
                    def _():
                        to_left(n - h, back).start()
                to_pair(n - h, back).start()
            for q in range(chunks):
                to_pair(h, q).wait_recv()
                to_pair(n - h, chunks - 1 - q).wait_recv()

        @pl.when(h == half)
        def _():
            for q in range(chunks // 2):
                back = chunks - 1 - q
                to_right(half - 1, q).wait_recv()
                to_pair(half, q).start()
                to_left(half + 1, back).wait_recv()
                to_pair(half, back).start()
            for q in range(chunks):
                to_pair(half, q).wait_recv()

        both = jnp.where((h > 0) & (h < half), 2, 1)

        @pl.loop(0, both)
        def _(side):
            compute(h * (1 - side) + (n - h) * side)

        return carry

    lax.fori_loop(0, half + 1, step_body, 0)

    for h in range(half):
        for q in range(chunks):
            if h < half - 1 or q < chunks // 2:
                to_right(h, q).wait_send()
            if h < half - 1 or q >= chunks // 2:
                to_left(n - h, q, x_part(q) if h == 0 else None).wait_send()
    for slot in range(n):
        for q in range(chunks):
            to_pair(slot, q).wait_send()


def solution(mesh):
    n = mesh.shape["vir"]
    natural = ring_is_natural(mesh)
    grid = grid_of(mesh)

    def on_device(factors, occ_energy, vir_energy):
        occ_local, vir_local, aux = factors.shape
        dma = pltpu.SemaphoreType.DMA
        blocks = pltpu.VMEM((n, 2 * occ_local, vir_local, aux), jnp.bfloat16)
        if grid and aux % 512 == 0 and vir_local % 128 == 0:
            parts = 8
            chunks, tiles = occ_local * parts, 4
            body = functools.partial(grid_kernel, chunks // 2)
            scratch = [
                blocks,
                pltpu.VMEM((occ_local, vir_local, aux), jnp.float32),
                pltpu.VMEM((occ_local, vir_local, aux), jnp.bfloat16),
                pltpu.VMEM((occ_local, vir_local, aux), jnp.bfloat16),
                pltpu.VMEM((3, occ_local * vir_local, 2 * occ_local * vir_local), jnp.bfloat16),
                dma,
                *[dma((3, chunks))] * 2,
                *[dma((2, chunks))] * 2,
                *[dma((3, chunks))] * 2,
                *[dma((n, parts))] * 2,
                *[dma((tiles, occ_local))] * 2,
                *[dma((3,))] * 2,
            ]
        else:
            chunks = 4
            body = functools.partial(kernel, n, natural, chunks)
            scratch = [
                blocks,
                dma,
                *[dma((n // 2, chunks)), dma((n // 2 + 1, chunks))] * 2,
                *[dma((n, chunks))] * 2,
            ]
        return pl.pallas_call(
            body,
            out_shape=pltpu.VMEM((occ_local, vir_local, aux), jnp.float32),
            in_specs=[
                pl.BlockSpec(memory_space=pl.ANY),
                pl.BlockSpec(memory_space=pltpu.SMEM),
                pl.BlockSpec(memory_space=pltpu.VMEM),
            ],
            out_specs=pl.BlockSpec(memory_space=pltpu.VMEM),
            scratch_shapes=scratch,
            compiler_params=pltpu.CompilerParams(
                collective_id=0, has_side_effects=True, vmem_limit_bytes=56 * 1024 * 1024
            ),
            name="ring_density",
        )(pltpu.with_memory_space_constraint(factors, pltpu.HBM), occ_energy, vir_energy.reshape(n, vir_local))

    return jax.shard_map(
        on_device,
        mesh=mesh,
        in_specs=(P(("frag", "occ"), "vir", None), P("frag"), P("frag")),
        out_specs=P(("frag", "occ"), "vir", None),
        check_vma=False,
    )
```

```python
import functools

import jax
import jax.numpy as jnp
from jax import lax
from jax.experimental import pallas as pl
from jax.experimental.pallas import tpu as pltpu
from jax.sharding import PartitionSpec as P

MESH = pl.DeviceIdType.MESH
energy_unit = 1.0 / 1024.0
NT = (((1,), (1,)), ((), ()))


def ring_is_natural(mesh):
    axis = list(mesh.axis_names).index("vir")
    devices = mesh.devices.swapaxes(axis, -1)
    line = devices.reshape(-1, devices.shape[-1])[0]
    coords = [getattr(d, "coords", None) for d in line]
    if any(c is None for c in coords):
        return False
    return all(
        sum(abs(p - q) for p, q in zip(a, b)) <= 1 for a, b in zip(coords, coords[1:])
    )


def grid_of(mesh):
    axis = list(mesh.axis_names).index("vir")
    devices = mesh.devices.swapaxes(axis, -1)
    line = devices.reshape(-1, devices.shape[-1])[0]
    coords = [getattr(d, "coords", None) for d in line]
    if len(line) != 8 or any(c is None for c in coords):
        return False

    def near(a, b):
        return sum(abs(p - q) for p, q in zip(coords[a], coords[b])) == 1

    return all(near(k, k + 1) for k in range(0, 8, 2)) and all(near(k, k + 2) for k in range(6))


def pair_amplitude(buf, a_slot, b_slot, base, own_occ, pair_occ, occ_local, vir_local, aux):
    wide = occ_local * vir_local
    here_own = buf[a_slot, 0:occ_local].reshape(wide, aux)
    here_all = buf[a_slot].reshape(2 * wide, aux)
    there_own = buf[b_slot, 0:occ_local].reshape(wide, aux)
    there_pair = buf[b_slot, occ_local:].reshape(wide, aux)
    with_own = lax.dot_general(
        here_all, there_own, NT, preferred_element_type=jnp.float32
    ).astype(jnp.bfloat16).astype(jnp.float32)
    with_pair = lax.dot_general(
        here_own, there_pair, NT, preferred_element_type=jnp.float32
    ).astype(jnp.bfloat16).astype(jnp.float32)

    def block(values, i, j):
        return values[i * vir_local:(i + 1) * vir_local, j * vir_local:(j + 1) * vir_local]

    bands = []
    for i in range(occ_local):
        band = []
        for j in range(occ_local):
            divisor = ((own_occ[i] + own_occ[j]) - base) * energy_unit
            band.append((2.0 * block(with_own, i, j) - block(with_own, j, i)) / divisor)
        for j in range(occ_local):
            divisor = ((own_occ[i] + pair_occ[j]) - base) * energy_unit
            crossed = block(with_own, occ_local + j, i)
            band.append((2.0 * block(with_pair, i, j) - crossed) / divisor)
        bands.append(jnp.concatenate(band, axis=1))
    return jnp.concatenate(bands, axis=0).astype(jnp.bfloat16)


def half_amplitude(buf, a_slot, b_slot, h, a_column, b_row, own_occ, pair_occ, occ_local, vir_local,
                   aux):
    wide, half = occ_local * vir_local, vir_local // 2
    here_own = buf[a_slot, 0:occ_local].reshape(wide, aux)
    here_all = buf[a_slot].reshape(2 * wide, aux)
    rows = pl.ds(pl.multiple_of(h * half, half), half)
    there_own = buf[b_slot, 0:occ_local, rows].reshape(occ_local * half, aux)
    there_pair = buf[b_slot, occ_local:, rows].reshape(occ_local * half, aux)
    with_own = lax.dot_general(
        here_all, there_own, NT, preferred_element_type=jnp.float32
    ).astype(jnp.bfloat16).astype(jnp.float32)
    with_pair = lax.dot_general(
        here_own, there_pair, NT, preferred_element_type=jnp.float32
    ).astype(jnp.bfloat16).astype(jnp.float32)

    low = lax.broadcasted_iota(jnp.int32, (1, vir_local), 1) < half

    def swap(values):
        return pltpu.roll(values, half, 1)

    def band(k):
        return with_own[k * vir_local:(k + 1) * vir_local]

    turned = swap(b_row)
    first = jnp.where(h == 0, b_row, turned)
    second = jnp.where(h == 0, turned, b_row)
    base = a_column + jnp.where(low, first, second)
    own_row = jnp.where(low, own_occ[0], own_occ[1])
    pair_row = jnp.where(low, pair_occ[0], pair_occ[1])
    bands = []
    for i in range(2):
        if i == 0:
            crossed = jnp.where(low, band(0), swap(band(1)))
            crossed_pair = jnp.where(low, band(2), swap(band(3)))
        else:
            crossed = jnp.where(low, swap(band(0)), band(1))
            crossed_pair = jnp.where(low, swap(band(2)), band(3))
        direct_pair = with_pair[i * vir_local:(i + 1) * vir_local]
        divisor = ((own_occ[i] + own_row) - base) * energy_unit
        divisor_pair = ((own_occ[i] + pair_row) - base) * energy_unit
        bands.append(jnp.concatenate([
            (2.0 * band(i) - crossed) / divisor, (2.0 * direct_pair - crossed_pair) / divisor_pair
        ], axis=1))
    return jnp.concatenate(bands, axis=0).astype(jnp.bfloat16)


E0, E1, M0, M1, F0, F1, G0, G1 = range(8)


def pick(s, table, default=-1):
    value = default
    for step, entry in table.items():
        value = jnp.where(s == step, entry, value)
    return value


def grid_kernel(share, early, lead, x_ref, occ_ref, vir_ref, out_ref, buf, sum_acc, sum_out, sum_in, amp,
                given_amp, local_sem, row_send, row_recv, end_send, end_recv, mid_send, mid_recv,
                pair_send, pair_recv, sum_send, sum_recv, amp_send, amp_recv):
    occ_local, vir_local, aux = x_ref.shape
    parts = row_send.shape[1] // occ_local
    rows = vir_local // parts
    chunks = parts * occ_local
    tiles = sum_send.shape[0]
    step = aux // tiles
    half_parts = parts // 2
    half = vir_local // 2
    cut = early * step
    core = lax.axis_index("occ")
    me = lax.axis_index("vir")
    pair = 1 - core
    column, row = me // 2, me % 2
    side = column // 2
    is_mid = (column + side) % 2
    mid, end = is_mid == 1, is_mid == 0

    def name_to_vir(slot):
        at, flip = slot // 2, slot % 2
        column_at = (1 - side) * at + side * (3 - at)
        return 2 * column_at + row + flip - 2 * row * flip

    other_row = 2 * column + 1 - row
    along = 2 * (is_mid * (3 * side) + (1 - is_mid) * (1 + side)) + row
    across = 2 * (3 - column) + row

    barrier = pltpu.get_barrier_semaphore()
    for target in ({"vir": other_row}, {"vir": along}, {"occ": pair}):
        pl.semaphore_signal(barrier, inc=1, device_id=target, device_id_type=MESH)

    @pl.when(mid)
    def _():
        pl.semaphore_signal(barrier, inc=1, device_id={"vir": across}, device_id_type=MESH)

    pl.semaphore_wait(barrier, 3 + is_mid)

    def part(slot, c, few=False):
        where = (slot, c % occ_local, pl.ds((c // occ_local) * rows, rows))
        return buf.at[where + ((pl.ds(0, cut),) if few else ())]

    def x_part(c):
        return x_ref.at[c % occ_local, pl.ds((c // occ_local) * rows, rows)]

    def copy(src, dst, sends, recvs, order, c, target):
        return pltpu.make_async_remote_copy(
            src_ref=src, dst_ref=dst, send_sem=sends.at[order, c], recv_sem=recvs.at[order, c],
            device_id=target, device_id_type=MESH,
        )

    def to_row(order, slot, c, src=None, few=False):
        there = slot + 1 - 2 * (slot % 2)
        return copy(part(slot, c, few) if src is None else src, part(there, c, few),
                    row_send, row_recv, order, c, {"vir": other_row})

    def to_end(order, slot, c, src=None, few=False):
        return copy(part(slot, c, few) if src is None else src, part(slot, c, few),
                    end_send, end_recv, order, c, {"vir": along})

    def to_mid(order, slot, c, src=None):
        there = 6 - 2 * (slot // 2) + slot % 2
        return copy(part(slot, c) if src is None else src, part(there, c),
                    mid_send, mid_recv, order, c, {"vir": across})

    def to_pair(slot, q, few=False):
        tail = (pl.ds(q * rows, rows),) + ((pl.ds(0, cut),) if few else ())
        return copy(buf.at[(slot, pl.ds(0, occ_local)) + tail],
                    buf.at[(slot, pl.ds(occ_local, occ_local)) + tail],
                    pair_send, pair_recv, slot, q, {"occ": pair})

    def to_sum(t):
        where = (pl.ds(0, occ_local), pl.ds(0, vir_local), pl.ds(t * step, step))
        return pltpu.make_async_remote_copy(
            src_ref=sum_out.at[where], dst_ref=sum_in.at[where], send_sem=sum_send.at[t],
            recv_sem=sum_recv.at[t], device_id={"vir": along}, device_id_type=MESH,
        )

    def to_amp(k, h):
        return copy(given_amp.at[k, h], given_amp.at[k, h], amp_send, amp_recv, k, h,
                    {"vir": along})

    own = is_mid * M0 + (1 - is_mid) * E0
    own_copy = pltpu.make_async_copy(x_ref, buf.at[own, pl.ds(0, occ_local)], local_sem)

    @pl.when(mid)
    def _():
        for c in range(lead):
            to_mid(1, M0, c, x_part(c)).start()

    @pl.loop(0, chunks)
    def _(c):
        @pl.when(end)
        def _():
            to_end(0, E0, c, x_part(c)).start()

        to_row(0, own, c, x_part(c)).start()

    own_copy.start()
    out_ref[...] = jnp.zeros_like(out_ref)

    @pl.when(mid)
    def _():
        sum_acc[...] = jnp.zeros_like(sum_acc)

    own_copy.wait()

    @pl.loop(0, parts)
    def _(q):
        to_pair(own, q).start()

    diagonal = lax.broadcasted_iota(jnp.int32, (vir_local, vir_local), 0) == (
        lax.broadcasted_iota(jnp.int32, (vir_local, vir_local), 1)
    )
    own_occ = [occ_ref[core * occ_local + i].astype(jnp.float32) for i in range(occ_local)]
    pair_occ = [occ_ref[pair * occ_local + i].astype(jnp.float32) for i in range(occ_local)]

    def energies(slot):
        return vir_ref[pl.ds(name_to_vir(slot), 1), :].astype(jnp.float32)

    def column_of(slot):
        return jnp.sum(jnp.where(diagonal, energies(slot), 0.0), axis=1, keepdims=True)

    def tile(t, width):
        return pl.ds(pl.multiple_of(t * width, width), width)

    def product(amplitude, b_slot, columns, width):
        there = buf[b_slot, :, :, columns].reshape(2 * occ_local * vir_local, width)
        piece = jnp.dot(amplitude, there, preferred_element_type=jnp.float32)
        return piece.reshape(occ_local, vir_local, width)

    def half_product(k, h, columns):
        rows_h = pl.ds(pl.multiple_of(h * half, half), half)
        there = buf[F0 + k, :, rows_h, columns].reshape(2 * occ_local * half, step)
        piece = jnp.dot(given_amp[k, h], there, preferred_element_type=jnp.float32)
        return piece.reshape(occ_local, vir_local, step)

    def send_sum(t):
        columns = tile(t, step)
        sum_out[:, :, columns] = sum_acc[:, :, columns].astype(jnp.bfloat16)
        to_sum(t).start()

    wide_step = 1024 if aux % 1024 == 0 else aux

    def arrive(role, s, first, count, body, order=None):
        @pl.when(role & (s >= first) & (s < first + count))
        def _():
            c = s - first
            body(c if order is None else order(c))

    def pair_on(slot, c, last=occ_local - 1, few=False):
        @pl.when(c % occ_local == last)
        def _():
            to_pair(slot, c // occ_local, few).start()

    turn = chunks + 2
    wait_far = max(lead, 2)
    close = 2 * chunks + 1
    last = close + 2 + chunks - share

    def mid_arrivals(s):
        def e0(c):
            to_end(0, E0, c).wait_recv()
            to_mid(0, E0, c).start()
            pair_on(E0, c)

        def g0(c):
            to_mid(0, E0, c).wait_recv()
            to_end(0, G0, c).start()
            pair_on(G0, c)

        def m1(c):
            to_row(0, M0, c).wait_recv()
            pair_on(M1, c)

        def own_rest(_):
            @pl.loop(lead, chunks)
            def _(c):
                to_mid(1, M0, c, x_part(c)).start()

        def f0(c):
            to_mid(1, M0, c).wait_recv()
            to_end(1, F0, c, few=True).start()
            to_row(1, F0, c).start()
            pair_on(F0, c)

        def f1(c):
            to_row(1, F0, c).wait_recv()
            pair_on(F1, c)

        def g0_first(_):
            to_row(2, G0, share).start()

        def g0_row(_):
            @pl.loop(share + 1, chunks)
            def _(c):
                to_row(2, G0, c).start()

        def e1(c):
            to_end(1, E1, c).wait_recv()

            @pl.when(c < share)
            def _():
                to_mid(2, E1, c).start()

            pair_on(E1, c)

        def g1(c):
            to_row(2, G0, c).wait_recv()
            pair_on(G1, c)

        def g1_rest(_):
            @pl.loop(0, share)
            def _(c):
                to_mid(2, E1, c).wait_recv()
                pair_on(G1, c)

        arrive(mid, s, 0, chunks, e0)
        arrive(mid, s, chunks - 1, 1, own_rest)
        arrive(mid, s, 1, lead, f0)
        arrive(mid, s, wait_far, chunks, g0)
        arrive(mid, s, 1, chunks, m1)
        arrive(mid, s, turn - 1 + lead, chunks - lead, f0, lambda c: c + lead)
        arrive(mid, s, turn + 1, chunks, f1)
        arrive(mid, s, turn - 1, 1, g0_first)
        arrive(mid, s, close, 1, g0_row)
        arrive(mid, s, turn, chunks, e1)
        arrive(mid, s, close + 2, chunks - share, g1, lambda c: c + share)
        arrive(mid, s, last, 1, g1_rest)

    def end_arrivals(s):
        def e1(c):
            to_row(0, E0, c).wait_recv()
            to_end(1, E1, c).start()
            pair_on(E1, c)

        def g0(c):
            to_end(0, G0, c).wait_recv()
            to_row(1, G0, c).start()
            pair_on(G0, c)

        def f0(c):
            to_end(1, F0, c, few=True).wait_recv()
            to_row(2, F0, c, few=True).start()
            pair_on(F0, c, few=True)

        def g1(c):
            to_row(1, G0, c).wait_recv()
            pair_on(G1, c)

        def f1(c):
            to_row(2, F0, c, few=True).wait_recv()
            pair_on(F1, c, few=True)

        arrive(end, s, 1, chunks, e1)
        arrive(end, s, 3, lead, f0)
        arrive(end, s, wait_far + 2, chunks, g0)
        arrive(end, s, turn + 2 + lead, chunks - lead, f0, lambda c: c + lead)
        arrive(end, s, turn + 1, chunks, g1)
        arrive(end, s, turn + 9, chunks, f1)

    first_half, second_half = chunks // 2 - 1, chunks - 1
    mid_for_end = {chunks: M0, turn: M1}
    mid_half = {turn + first_half + 1: 0, turn + first_half + 4: 2, close: 1, close + 2: 3}
    mid_own = {turn + 2: M0, turn + 4: E0, turn + 6: M1, turn + 9: G0, close + 3: F0,
               close + 4: F1, close + 5: E1, last: G1}
    end_own = {2: E0, turn: E1, turn + 3: G0, close + 3: G1}
    end_half = {close + 4: 0, close + 6: 2, close + 8: 1, close + 10: 3}
    steps = max(last + 1, close + 10) + 1

    def one(s, carry):
        mid_arrivals(s)
        end_arrivals(s)
        def jobs(at):
            return (is_mid * (pick(at, mid_for_end) + 1) - 1,
                    is_mid * pick(at, mid_own) + (1 - is_mid) * pick(at, end_own))

        code = is_mid * pick(s, mid_half) + (1 - is_mid) * pick(s, end_half)
        k, h = code // 2, code % 2
        for_end, for_own = jobs(s - 1)

        @pl.when(for_own >= 0)
        def _():
            @pl.loop(0, aux // wide_step)
            def _(t):
                columns = tile(t, wide_step)
                out_ref[:, :, columns] += product(amp[...], for_own, columns, wide_step)

        @pl.when(for_end >= 0)
        def _():
            @pl.loop(0, tiles)
            def _(t):
                columns = tile(t, step)
                sum_acc[:, :, columns] += product(amp[...], for_end, columns, step)

                @pl.when((for_end == M1) & (t < early))
                def _():
                    send_sum(t)

        next_for_end, next_for_own = jobs(s)
        b_slot = jnp.maximum(next_for_end, next_for_own)
        new = end | (next_for_end >= 0) | (b_slot == G0) | (b_slot == E1) | (b_slot == G1)

        @pl.when((b_slot >= 0) & new)
        def _():
            @pl.loop(0, parts)
            def _(q):
                to_pair(b_slot, q).wait_recv()

        @pl.when(mid & (s == chunks))
        def _():
            @pl.loop(0, parts)
            def _(q):
                to_pair(E0, q).wait_recv()

        @pl.when(b_slot >= 0)
        def _():
            a_slot = jnp.where(next_for_end >= 0, E0, own)
            base = column_of(a_slot) + energies(b_slot)
            amp[...] = pair_amplitude(
                buf, a_slot, b_slot, base, own_occ, pair_occ, occ_local, vir_local, aux
            )

        @pl.when(mid & (code >= 0))
        def _():
            @pl.loop(h * half_parts, (h + 1) * half_parts)
            def _(q):
                to_pair(F0 + k, q).wait_recv()

            given_amp[k, h] = half_amplitude(
                buf, E0, F0 + k, h, column_of(E0), energies(F0 + k), own_occ, pair_occ,
                occ_local, vir_local, aux,
            )
            to_amp(k, h).start()

            @pl.loop(early, tiles)
            def _(t):
                columns = tile(t, step)
                sum_acc[:, :, columns] += half_product(k, h, columns)

                @pl.when(code == 3)
                def _():
                    send_sum(t)

        @pl.when(end & (code >= 0))
        def _():
            to_amp(k, h).wait_recv()

            @pl.loop(h * half_parts, (h + 1) * half_parts)
            def _(q):
                to_pair(F0 + k, q, few=True).wait_recv()

            @pl.loop(0, early)
            def _(t):
                columns = tile(t, step)
                out_ref[:, :, columns] += half_product(k, h, columns)

        return carry

    lax.fori_loop(0, steps, one, 0)

    @pl.when(end)
    def _():
        @pl.loop(0, tiles)
        def _(t):
            columns = tile(t, step)
            to_sum(t).wait_recv()
            out_ref[:, :, columns] += sum_in[:, :, columns].astype(jnp.float32)

    @pl.loop(0, chunks)
    def _(c):
        to_row(0, own, c, x_part(c)).wait_send()
        to_row(1, F0, c).wait_send()
        to_end(0, E0, c).wait_send()

        @pl.when(mid)
        def _():
            to_end(1, F0, c, few=True).wait_send()
            to_mid(0, E0, c).wait_send()
            to_mid(1, M0, c, x_part(c)).wait_send()

            @pl.when(c >= share)
            def _():
                to_row(2, G0, c).wait_send()

            @pl.when(c < share)
            def _():
                to_mid(2, E1, c).wait_send()

        @pl.when(end)
        def _():
            to_end(1, E1, c).wait_send()
            to_row(2, F0, c, few=True).wait_send()

    @pl.loop(0, parts)
    def _(q):
        for slot in (E0, E1, G0, G1):
            to_pair(slot, q).wait_send()

        for slot in (M0, M1):
            @pl.when(mid)
            def _():
                to_pair(slot, q).wait_send()

        for slot in (F0, F1):
            @pl.when(mid)
            def _():
                to_pair(slot, q).wait_send()

            @pl.when(end)
            def _():
                to_pair(slot, q, few=True).wait_send()

    @pl.when(mid)
    def _():
        for k in range(2):
            for h in range(2):
                to_amp(k, h).wait_send()

        @pl.loop(0, tiles)
        def _(t):
            to_sum(t).wait_send()


def kernel(n, natural, chunks, x_ref, occ_ref, vir_ref, out_ref, buf, local_sem,
           right_send, right_recv, left_send, left_recv, pair_send, pair_recv):
    occ_local, vir_local, aux = x_ref.shape
    half = n // 2
    rows = vir_local // chunks
    core = lax.axis_index("occ")
    me = lax.axis_index("vir")

    if natural:
        place = me

        def at_place(k):
            return k
    else:
        odd = me % 2
        place = (1 - odd) * (me // 2) + odd * (n - 1 - me // 2)

        def at_place(k):
            down = k // half
            return (1 - down) * (2 * k) + down * (2 * (n - k) - 1)

    right = at_place((place + 1) % n)
    left = at_place((place + n - 1) % n)
    pair = 1 - core

    barrier = pltpu.get_barrier_semaphore()
    for target in ({"vir": right}, {"vir": left}, {"occ": pair}):
        pl.semaphore_signal(barrier, inc=1, device_id=target, device_id_type=MESH)
    pl.semaphore_wait(barrier, 3)

    def own_part(slot, q):
        return buf.at[slot, pl.ds(0, occ_local), pl.ds(q * rows, rows)]

    def pair_part(slot, q):
        return buf.at[slot, pl.ds(occ_local, occ_local), pl.ds(q * rows, rows)]

    def to_right(slot, q, src=None):
        return pltpu.make_async_remote_copy(
            src_ref=own_part(slot, q) if src is None else src,
            dst_ref=own_part(slot + 1, q),
            send_sem=right_send.at[slot, q],
            recv_sem=right_recv.at[slot + 1, q],
            device_id={"vir": right},
            device_id_type=MESH,
        )

    def to_left(slot, q, src=None):
        return pltpu.make_async_remote_copy(
            src_ref=own_part(slot % n, q) if src is None else src,
            dst_ref=own_part(slot - 1, q),
            send_sem=left_send.at[n - slot, q],
            recv_sem=left_recv.at[n - slot + 1, q],
            device_id={"vir": left},
            device_id_type=MESH,
        )

    def to_pair(slot, q, src=None):
        return pltpu.make_async_remote_copy(
            src_ref=own_part(slot, q) if src is None else src,
            dst_ref=pair_part(slot, q),
            send_sem=pair_send.at[slot, q],
            recv_sem=pair_recv.at[slot, q],
            device_id={"occ": pair},
            device_id_type=MESH,
        )

    def x_part(q):
        return x_ref.at[:, pl.ds(q * rows, rows)]

    own_copy = pltpu.make_async_copy(x_ref, buf.at[0, pl.ds(0, occ_local)], local_sem)
    for q in range(chunks):
        to_right(0, q, x_part(q)).start()
        to_left(n, chunks - 1 - q, x_part(chunks - 1 - q)).start()
    own_copy.start()
    for q in range(chunks):
        to_pair(0, q, x_part(q)).start()
    out_ref[...] = jnp.zeros_like(out_ref)
    own_copy.wait()

    diagonal = lax.broadcasted_iota(jnp.int32, (vir_local, vir_local), 0) == (
        lax.broadcasted_iota(jnp.int32, (vir_local, vir_local), 1)
    )
    own_row = vir_ref[pl.ds(me, 1), :].astype(jnp.float32)
    own_column = jnp.sum(jnp.where(diagonal, own_row, 0.0), axis=1, keepdims=True)
    own_occ = [occ_ref[core * occ_local + i].astype(jnp.float32) for i in range(occ_local)]
    pair_occ = [occ_ref[pair * occ_local + i].astype(jnp.float32) for i in range(occ_local)]

    def compute(slot):
        source = at_place((place - slot + n) % n)
        energy_row = vir_ref[pl.ds(source, 1), :].astype(jnp.float32)
        base = own_column + energy_row
        amplitude = pair_amplitude(
            buf, 0, slot, base, own_occ, pair_occ, occ_local, vir_local, aux
        )

        step = 1024 if aux % 1024 == 0 else aux

        @pl.loop(0, aux // step)
        def _(t):
            columns = pl.ds(pl.multiple_of(t * step, step), step)
            there = buf[slot, :, :, columns].reshape(2 * occ_local * vir_local, step)
            part = jnp.dot(amplitude, there, preferred_element_type=jnp.float32)
            out_ref[:, :, columns] += part.reshape(occ_local, vir_local, step)

    def step_body(h, carry):
        @pl.when(h == 0)
        def _():
            for q in range(chunks):
                to_pair(0, q).wait_recv()

        @pl.when((h > 0) & (h < half))
        def _():
            for q in range(chunks):
                back = chunks - 1 - q
                to_right(h - 1, q).wait_recv()
                if q < chunks // 2:
                    to_right(h, q).start()
                else:
                    @pl.when(h < half - 1)
                    def _():
                        to_right(h, q).start()
                to_pair(h, q).start()
                to_left(n - h + 1, back).wait_recv()
                if back >= chunks // 2:
                    to_left(n - h, back).start()
                else:
                    @pl.when(h < half - 1)
                    def _():
                        to_left(n - h, back).start()
                to_pair(n - h, back).start()
            for q in range(chunks):
                to_pair(h, q).wait_recv()
                to_pair(n - h, chunks - 1 - q).wait_recv()

        @pl.when(h == half)
        def _():
            for q in range(chunks // 2):
                back = chunks - 1 - q
                to_right(half - 1, q).wait_recv()
                to_pair(half, q).start()
                to_left(half + 1, back).wait_recv()
                to_pair(half, back).start()
            for q in range(chunks):
                to_pair(half, q).wait_recv()

        both = jnp.where((h > 0) & (h < half), 2, 1)

        @pl.loop(0, both)
        def _(side):
            compute(h * (1 - side) + (n - h) * side)

        return carry

    lax.fori_loop(0, half + 1, step_body, 0)

    for h in range(half):
        for q in range(chunks):
            if h < half - 1 or q < chunks // 2:
                to_right(h, q).wait_send()
            if h < half - 1 or q >= chunks // 2:
                to_left(n - h, q, x_part(q) if h == 0 else None).wait_send()
    for slot in range(n):
        for q in range(chunks):
            to_pair(slot, q).wait_send()


def solution(mesh):
    n = mesh.shape["vir"]
    natural = ring_is_natural(mesh)
    grid = grid_of(mesh)

    def on_device(factors, occ_energy, vir_energy):
        occ_local, vir_local, aux = factors.shape
        dma = pltpu.SemaphoreType.DMA
        blocks = pltpu.VMEM((n, 2 * occ_local, vir_local, aux), jnp.bfloat16)
        parts, tiles = 8, 12
        fits = occ_local == 2 and vir_local == 128 and aux % (tiles * 128) == 0
        if grid and fits:
            chunks, wide = occ_local * parts, occ_local * vir_local
            early, lead = 6, 2
            body = functools.partial(grid_kernel, chunks // 2, early, lead)
            scratch = [
                blocks,
                pltpu.VMEM((occ_local, vir_local, aux), jnp.float32),
                pltpu.VMEM((occ_local, vir_local, aux), jnp.bfloat16),
                pltpu.VMEM((occ_local, vir_local, aux), jnp.bfloat16),
                pltpu.VMEM((wide, 2 * wide), jnp.bfloat16),
                pltpu.VMEM((2, 2, wide, wide), jnp.bfloat16),
                dma,
                *[dma((3, chunks))] * 2,
                *[dma((2, chunks))] * 2,
                *[dma((3, chunks))] * 2,
                *[dma((n, parts))] * 2,
                *[dma((tiles,))] * 2,
                *[dma((2, 2))] * 2,
            ]
        else:
            chunks = 4
            body = functools.partial(kernel, n, natural, chunks)
            scratch = [
                blocks,
                dma,
                *[dma((n // 2, chunks)), dma((n // 2 + 1, chunks))] * 2,
                *[dma((n, chunks))] * 2,
            ]
        return pl.pallas_call(
            body,
            out_shape=pltpu.VMEM((occ_local, vir_local, aux), jnp.float32),
            in_specs=[
                pl.BlockSpec(memory_space=pl.ANY),
                pl.BlockSpec(memory_space=pltpu.SMEM),
                pl.BlockSpec(memory_space=pltpu.VMEM),
            ],
            out_specs=pl.BlockSpec(memory_space=pltpu.VMEM),
            scratch_shapes=scratch,
            compiler_params=pltpu.CompilerParams(
                collective_id=0, has_side_effects=True, vmem_limit_bytes=56 * 1024 * 1024
            ),
            name="ring_density",
        )(pltpu.with_memory_space_constraint(factors, pltpu.HBM), occ_energy, vir_energy.reshape(n, vir_local))

    return jax.shard_map(
        on_device,
        mesh=mesh,
        in_specs=(P(("frag", "occ"), "vir", None), P("frag"), P("frag")),
        out_specs=P(("frag", "occ"), "vir", None),
        check_vma=False,
    )
```

```python
import functools

import jax
import jax.numpy as jnp
from jax import lax
from jax.experimental import pallas as pl
from jax.experimental.pallas import tpu as pltpu
from jax.sharding import PartitionSpec as P

MESH = pl.DeviceIdType.MESH
energy_unit = 1.0 / 1024.0
NT = (((1,), (1,)), ((), ()))


def ring_is_natural(mesh):
    axis = list(mesh.axis_names).index("vir")
    devices = mesh.devices.swapaxes(axis, -1)
    line = devices.reshape(-1, devices.shape[-1])[0]
    coords = [getattr(d, "coords", None) for d in line]
    if any(c is None for c in coords):
        return False
    return all(
        sum(abs(p - q) for p, q in zip(a, b)) <= 1 for a, b in zip(coords, coords[1:])
    )


def grid_of(mesh):
    axis = list(mesh.axis_names).index("vir")
    devices = mesh.devices.swapaxes(axis, -1)
    line = devices.reshape(-1, devices.shape[-1])[0]
    coords = [getattr(d, "coords", None) for d in line]
    if len(line) != 8 or any(c is None for c in coords):
        return False

    def near(a, b):
        return sum(abs(p - q) for p, q in zip(coords[a], coords[b])) == 1

    return all(near(k, k + 1) for k in range(0, 8, 2)) and all(near(k, k + 2) for k in range(6))


def pair_amplitude(buf, a_slot, b_slot, base, own_occ, pair_occ, occ_local, vir_local, aux):
    wide = occ_local * vir_local
    here_own = buf[a_slot, 0:occ_local].reshape(wide, aux)
    here_all = buf[a_slot].reshape(2 * wide, aux)
    there_own = buf[b_slot, 0:occ_local].reshape(wide, aux)
    there_pair = buf[b_slot, occ_local:].reshape(wide, aux)
    with_own = lax.dot_general(
        here_all, there_own, NT, preferred_element_type=jnp.float32
    ).astype(jnp.bfloat16).astype(jnp.float32)
    with_pair = lax.dot_general(
        here_own, there_pair, NT, preferred_element_type=jnp.float32
    ).astype(jnp.bfloat16).astype(jnp.float32)

    def block(values, i, j):
        return values[i * vir_local:(i + 1) * vir_local, j * vir_local:(j + 1) * vir_local]

    bands = []
    for i in range(occ_local):
        band = []
        for j in range(occ_local):
            divisor = ((own_occ[i] + own_occ[j]) - base) * energy_unit
            band.append((2.0 * block(with_own, i, j) - block(with_own, j, i)) / divisor)
        for j in range(occ_local):
            divisor = ((own_occ[i] + pair_occ[j]) - base) * energy_unit
            crossed = block(with_own, occ_local + j, i)
            band.append((2.0 * block(with_pair, i, j) - crossed) / divisor)
        bands.append(jnp.concatenate(band, axis=1))
    return jnp.concatenate(bands, axis=0).astype(jnp.bfloat16)


def half_amplitude(buf, a_slot, b_slot, h, a_column, b_row, own_occ, pair_occ, occ_local, vir_local,
                   aux):
    wide, half = occ_local * vir_local, vir_local // 2
    here_own = buf[a_slot, 0:occ_local].reshape(wide, aux)
    here_all = buf[a_slot].reshape(2 * wide, aux)
    rows = pl.ds(pl.multiple_of(h * half, half), half)
    there_own = buf[b_slot, 0:occ_local, rows].reshape(occ_local * half, aux)
    there_pair = buf[b_slot, occ_local:, rows].reshape(occ_local * half, aux)
    with_own = lax.dot_general(
        here_all, there_own, NT, preferred_element_type=jnp.float32
    ).astype(jnp.bfloat16).astype(jnp.float32)
    with_pair = lax.dot_general(
        here_own, there_pair, NT, preferred_element_type=jnp.float32
    ).astype(jnp.bfloat16).astype(jnp.float32)

    low = lax.broadcasted_iota(jnp.int32, (1, vir_local), 1) < half

    def swap(values):
        return pltpu.roll(values, half, 1)

    def band(k):
        return with_own[k * vir_local:(k + 1) * vir_local]

    turned = swap(b_row)
    first = jnp.where(h == 0, b_row, turned)
    second = jnp.where(h == 0, turned, b_row)
    base = a_column + jnp.where(low, first, second)
    own_row = jnp.where(low, own_occ[0], own_occ[1])
    pair_row = jnp.where(low, pair_occ[0], pair_occ[1])
    bands = []
    for i in range(2):
        if i == 0:
            crossed = jnp.where(low, band(0), swap(band(1)))
            crossed_pair = jnp.where(low, band(2), swap(band(3)))
        else:
            crossed = jnp.where(low, swap(band(0)), band(1))
            crossed_pair = jnp.where(low, swap(band(2)), band(3))
        direct_pair = with_pair[i * vir_local:(i + 1) * vir_local]
        divisor = ((own_occ[i] + own_row) - base) * energy_unit
        divisor_pair = ((own_occ[i] + pair_row) - base) * energy_unit
        bands.append(jnp.concatenate([
            (2.0 * band(i) - crossed) / divisor, (2.0 * direct_pair - crossed_pair) / divisor_pair
        ], axis=1))
    return jnp.concatenate(bands, axis=0).astype(jnp.bfloat16)


E0, E1, M0, M1, F0, F1, G0, G1 = range(8)


def pick(s, table, default=-1):
    value = default
    for step, entry in table.items():
        value = jnp.where(s == step, entry, value)
    return value


def grid_kernel(share, early, lead, x_ref, occ_ref, vir_ref, out_ref, buf, sum_acc, sum_out, sum_in, amp,
                given_amp, local_sem, row_send, row_recv, end_send, end_recv, mid_send, mid_recv,
                pair_send, pair_recv, sum_send, sum_recv, amp_send, amp_recv):
    occ_local, vir_local, aux = x_ref.shape
    parts = row_send.shape[1] // occ_local
    rows = vir_local // parts
    chunks = parts * occ_local
    tiles = sum_send.shape[0]
    step = aux // tiles
    half_parts = parts // 2
    half = vir_local // 2
    cut = early * step
    core = lax.axis_index("occ")
    me = lax.axis_index("vir")
    pair = 1 - core
    column, row = me // 2, me % 2
    side = column // 2
    is_mid = (column + side) % 2
    mid, end = is_mid == 1, is_mid == 0

    def name_to_vir(slot):
        at, flip = slot // 2, slot % 2
        column_at = (1 - side) * at + side * (3 - at)
        return 2 * column_at + row + flip - 2 * row * flip

    other_row = 2 * column + 1 - row
    along = 2 * (is_mid * (3 * side) + (1 - is_mid) * (1 + side)) + row
    across = 2 * (3 - column) + row

    barrier = pltpu.get_barrier_semaphore()
    for target in ({"vir": other_row}, {"vir": along}, {"occ": pair}):
        pl.semaphore_signal(barrier, inc=1, device_id=target, device_id_type=MESH)

    @pl.when(mid)
    def _():
        pl.semaphore_signal(barrier, inc=1, device_id={"vir": across}, device_id_type=MESH)

    pl.semaphore_wait(barrier, 3 + is_mid)

    def part(slot, c, few=False):
        where = (slot, c % occ_local, pl.ds((c // occ_local) * rows, rows))
        return buf.at[where + ((pl.ds(0, cut),) if few else ())]

    def x_part(c):
        return x_ref.at[c % occ_local, pl.ds((c // occ_local) * rows, rows)]

    def copy(src, dst, sends, recvs, order, c, target):
        return pltpu.make_async_remote_copy(
            src_ref=src, dst_ref=dst, send_sem=sends.at[order, c], recv_sem=recvs.at[order, c],
            device_id=target, device_id_type=MESH,
        )

    def to_row(order, slot, c, src=None, few=False):
        there = slot + 1 - 2 * (slot % 2)
        return copy(part(slot, c, few) if src is None else src, part(there, c, few),
                    row_send, row_recv, order, c, {"vir": other_row})

    def to_end(order, slot, c, src=None, few=False):
        return copy(part(slot, c, few) if src is None else src, part(slot, c, few),
                    end_send, end_recv, order, c, {"vir": along})

    def to_mid(order, slot, c, src=None):
        there = 6 - 2 * (slot // 2) + slot % 2
        return copy(part(slot, c) if src is None else src, part(there, c),
                    mid_send, mid_recv, order, c, {"vir": across})

    def to_pair(slot, q, few=False):
        tail = (pl.ds(q * rows, rows),) + ((pl.ds(0, cut),) if few else ())
        return copy(buf.at[(slot, pl.ds(0, occ_local)) + tail],
                    buf.at[(slot, pl.ds(occ_local, occ_local)) + tail],
                    pair_send, pair_recv, slot, q, {"occ": pair})

    def to_sum(t):
        return pltpu.make_async_remote_copy(
            src_ref=sum_out.at[t], dst_ref=sum_in.at[t], send_sem=sum_send.at[t],
            recv_sem=sum_recv.at[t], device_id={"vir": along}, device_id_type=MESH,
        )

    def to_amp(k, h):
        return copy(given_amp.at[k, h], given_amp.at[k, h], amp_send, amp_recv, k, h,
                    {"vir": along})

    own = is_mid * M0 + (1 - is_mid) * E0
    own_copy = pltpu.make_async_copy(x_ref, buf.at[own, pl.ds(0, occ_local)], local_sem)

    @pl.when(mid)
    def _():
        for c in range(lead):
            to_mid(1, M0, c, x_part(c)).start()

    @pl.loop(0, chunks)
    def _(c):
        @pl.when(end)
        def _():
            to_end(0, E0, c, x_part(c)).start()

        to_row(0, own, c, x_part(c)).start()

    own_copy.start()
    out_ref[...] = jnp.zeros_like(out_ref)

    @pl.when(mid)
    def _():
        sum_acc[...] = jnp.zeros_like(sum_acc)

    own_copy.wait()

    @pl.loop(0, parts)
    def _(q):
        to_pair(own, q).start()

    diagonal = lax.broadcasted_iota(jnp.int32, (vir_local, vir_local), 0) == (
        lax.broadcasted_iota(jnp.int32, (vir_local, vir_local), 1)
    )
    own_occ = [occ_ref[core * occ_local + i].astype(jnp.float32) for i in range(occ_local)]
    pair_occ = [occ_ref[pair * occ_local + i].astype(jnp.float32) for i in range(occ_local)]

    def energies(slot):
        return vir_ref[pl.ds(name_to_vir(slot), 1), :].astype(jnp.float32)

    def column_of(slot):
        return jnp.sum(jnp.where(diagonal, energies(slot), 0.0), axis=1, keepdims=True)

    def tile(t, width):
        return pl.ds(pl.multiple_of(t * width, width), width)

    def product(b_slot, columns):
        there = buf[b_slot, :, :, columns].reshape(2 * occ_local * vir_local, columns.size)
        piece = jnp.dot(amp[...], there, preferred_element_type=jnp.float32)
        return piece.reshape(occ_local, vir_local, columns.size)

    def half_product(k, h, columns):
        rows_h = pl.ds(pl.multiple_of(h * half, half), half)
        there = buf[F0 + k, :, rows_h, columns].reshape(2 * occ_local * half, columns.size)
        piece = jnp.dot(given_amp[k, h], there, preferred_element_type=jnp.float32)
        return piece.reshape(occ_local, vir_local, columns.size)

    def send_sum(t):
        columns = tile(t, step)
        sum_out[t] = sum_acc[:, :, columns].astype(jnp.bfloat16)
        to_sum(t).start()

    low_columns, high_columns = pl.ds(0, cut), pl.ds(cut, aux - cut)

    def arrive(role, s, first, count, body, order=None):
        @pl.when(role & (s >= first) & (s < first + count))
        def _():
            c = s - first
            body(c if order is None else order(c))

    def pair_on(slot, c, last=occ_local - 1, few=False):
        @pl.when(c % occ_local == last)
        def _():
            to_pair(slot, c // occ_local, few).start()

    turn = chunks + 2
    wait_far = max(lead, 2)
    close = 2 * chunks + 1
    last = close + 2 + chunks - share

    def mid_arrivals(s):
        def e0(c):
            to_end(0, E0, c).wait_recv()
            to_mid(0, E0, c).start()
            pair_on(E0, c)

        def g0(c):
            to_mid(0, E0, c).wait_recv()
            to_end(0, G0, c).start()
            pair_on(G0, c)

        def m1(c):
            to_row(0, M0, c).wait_recv()
            pair_on(M1, c)

        def own_rest(_):
            @pl.loop(lead, chunks)
            def _(c):
                to_mid(1, M0, c, x_part(c)).start()

        def f0(c):
            to_mid(1, M0, c).wait_recv()
            to_end(1, F0, c, few=True).start()
            to_row(1, F0, c).start()
            pair_on(F0, c)

        def f1(c):
            to_row(1, F0, c).wait_recv()
            pair_on(F1, c)

        def g0_first(_):
            to_row(2, G0, share).start()

        def g0_row(_):
            @pl.loop(share + 1, chunks)
            def _(c):
                to_row(2, G0, c).start()

        def e1(c):
            to_end(1, E1, c).wait_recv()

            @pl.when(c < share)
            def _():
                to_mid(2, E1, c).start()

            pair_on(E1, c)

        def g1(c):
            to_row(2, G0, c).wait_recv()
            pair_on(G1, c)

        def g1_rest(_):
            @pl.loop(0, share)
            def _(c):
                to_mid(2, E1, c).wait_recv()
                pair_on(G1, c)

        arrive(mid, s, 0, chunks, e0)
        arrive(mid, s, chunks - 1, 1, own_rest)
        arrive(mid, s, 1, lead, f0)
        arrive(mid, s, wait_far, chunks, g0)
        arrive(mid, s, 1, chunks, m1)
        arrive(mid, s, turn - 1 + lead, chunks - lead, f0, lambda c: c + lead)
        arrive(mid, s, turn + 1, chunks, f1)
        arrive(mid, s, turn - 1, 1, g0_first)
        arrive(mid, s, close, 1, g0_row)
        arrive(mid, s, turn, chunks, e1)
        arrive(mid, s, close + 2, chunks - share, g1, lambda c: c + share)
        arrive(mid, s, last, 1, g1_rest)

    def end_arrivals(s):
        def e1(c):
            to_row(0, E0, c).wait_recv()
            to_end(1, E1, c).start()
            pair_on(E1, c)

        def g0(c):
            to_end(0, G0, c).wait_recv()
            to_row(1, G0, c).start()
            pair_on(G0, c)

        def f0(c):
            to_end(1, F0, c, few=True).wait_recv()
            to_row(2, F0, c, few=True).start()
            pair_on(F0, c, few=True)

        def g1(c):
            to_row(1, G0, c).wait_recv()
            pair_on(G1, c)

        def f1(c):
            to_row(2, F0, c, few=True).wait_recv()
            pair_on(F1, c, few=True)

        arrive(end, s, 1, chunks, e1)
        arrive(end, s, 3, lead, f0)
        arrive(end, s, wait_far + 2, chunks, g0)
        arrive(end, s, turn + 2 + lead, chunks - lead, f0, lambda c: c + lead)
        arrive(end, s, turn + 1, chunks, g1)
        arrive(end, s, turn + 9, chunks, f1)

    first_half, second_half = chunks // 2 - 1, chunks - 1
    mid_for_end = {chunks: M0, turn: M1}
    mid_half = {turn + first_half + 1: 0, turn + first_half + 3: 2, close: 1, close + 1: 3}
    mid_own = {turn + 3: M0, close + 2: E0, close + 3: M1, close + 4: G0, close + 5: F0, close + 6: F1, close + 7: E1, last: G1}
    end_own = {2: E0, turn: E1, turn + 3: G0, close + 3: G1}
    end_half = {close + 4: 0, close + 6: 2, close + 8: 1, close + 10: 3}
    steps = max(last + 1, close + 10) + 1

    def one(s, carry):
        mid_arrivals(s)
        end_arrivals(s)
        def jobs(at):
            return (is_mid * (pick(at, mid_for_end) + 1) - 1,
                    is_mid * pick(at, mid_own) + (1 - is_mid) * pick(at, end_own))

        code = is_mid * pick(s, mid_half) + (1 - is_mid) * pick(s, end_half)
        k, h = code // 2, code % 2
        for_end, for_own = jobs(s - 1)

        @pl.when(for_own >= 0)
        def _():
            out_ref[...] += product(for_own, pl.ds(0, aux))

        @pl.when(for_end >= 0)
        def _():
            sum_acc[:, :, low_columns] += product(for_end, low_columns)

            @pl.when(for_end == M1)
            def _():
                @pl.loop(0, early)
                def _(t):
                    send_sum(t)

            sum_acc[:, :, high_columns] += product(for_end, high_columns)

        next_for_end, next_for_own = jobs(s)
        b_slot = jnp.maximum(next_for_end, next_for_own)
        new = end | (next_for_end >= 0) | (b_slot == G0) | (b_slot == E1) | (b_slot == G1)

        @pl.when((b_slot >= 0) & new)
        def _():
            @pl.loop(0, parts)
            def _(q):
                to_pair(b_slot, q).wait_recv()

        @pl.when(mid & (s == chunks))
        def _():
            @pl.loop(0, parts)
            def _(q):
                to_pair(E0, q).wait_recv()

        @pl.when(b_slot >= 0)
        def _():
            a_slot = jnp.where(next_for_end >= 0, E0, own)
            base = column_of(a_slot) + energies(b_slot)
            amp[...] = pair_amplitude(
                buf, a_slot, b_slot, base, own_occ, pair_occ, occ_local, vir_local, aux
            )

        @pl.when(mid & (code >= 0))
        def _():
            @pl.loop(h * half_parts, (h + 1) * half_parts)
            def _(q):
                to_pair(F0 + k, q).wait_recv()

            given_amp[k, h] = half_amplitude(
                buf, E0, F0 + k, h, column_of(E0), energies(F0 + k), own_occ, pair_occ,
                occ_local, vir_local, aux,
            )
            to_amp(k, h).start()

            sum_acc[:, :, high_columns] += half_product(k, h, high_columns)

            @pl.when(code == 3)
            def _():
                @pl.loop(early, tiles)
                def _(t):
                    send_sum(t)

        @pl.when(end & (code >= 0))
        def _():
            to_amp(k, h).wait_recv()

            @pl.loop(h * half_parts, (h + 1) * half_parts)
            def _(q):
                to_pair(F0 + k, q, few=True).wait_recv()

            out_ref[:, :, low_columns] += half_product(k, h, low_columns)

        return carry

    lax.fori_loop(0, steps, one, 0)

    @pl.when(end)
    def _():
        @pl.loop(0, tiles)
        def _(t):
            columns = tile(t, step)
            to_sum(t).wait_recv()
            out_ref[:, :, columns] += sum_in[t].astype(jnp.float32)

    @pl.loop(0, chunks)
    def _(c):
        to_row(0, own, c, x_part(c)).wait_send()
        to_row(1, F0, c).wait_send()
        to_end(0, E0, c).wait_send()

        @pl.when(mid)
        def _():
            to_end(1, F0, c, few=True).wait_send()
            to_mid(0, E0, c).wait_send()
            to_mid(1, M0, c, x_part(c)).wait_send()

            @pl.when(c >= share)
            def _():
                to_row(2, G0, c).wait_send()

            @pl.when(c < share)
            def _():
                to_mid(2, E1, c).wait_send()

        @pl.when(end)
        def _():
            to_end(1, E1, c).wait_send()
            to_row(2, F0, c, few=True).wait_send()

    @pl.loop(0, parts)
    def _(q):
        for slot in (E0, E1, G0, G1):
            to_pair(slot, q).wait_send()

        for slot in (M0, M1):
            @pl.when(mid)
            def _():
                to_pair(slot, q).wait_send()

        for slot in (F0, F1):
            @pl.when(mid)
            def _():
                to_pair(slot, q).wait_send()

            @pl.when(end)
            def _():
                to_pair(slot, q, few=True).wait_send()

    @pl.when(mid)
    def _():
        for k in range(2):
            for h in range(2):
                to_amp(k, h).wait_send()

        @pl.loop(0, tiles)
        def _(t):
            to_sum(t).wait_send()


def kernel(n, natural, chunks, x_ref, occ_ref, vir_ref, out_ref, buf, local_sem,
           right_send, right_recv, left_send, left_recv, pair_send, pair_recv):
    occ_local, vir_local, aux = x_ref.shape
    half = n // 2
    rows = vir_local // chunks
    core = lax.axis_index("occ")
    me = lax.axis_index("vir")

    if natural:
        place = me

        def at_place(k):
            return k
    else:
        odd = me % 2
        place = (1 - odd) * (me // 2) + odd * (n - 1 - me // 2)

        def at_place(k):
            down = k // half
            return (1 - down) * (2 * k) + down * (2 * (n - k) - 1)

    right = at_place((place + 1) % n)
    left = at_place((place + n - 1) % n)
    pair = 1 - core

    barrier = pltpu.get_barrier_semaphore()
    for target in ({"vir": right}, {"vir": left}, {"occ": pair}):
        pl.semaphore_signal(barrier, inc=1, device_id=target, device_id_type=MESH)
    pl.semaphore_wait(barrier, 3)

    def own_part(slot, q):
        return buf.at[slot, pl.ds(0, occ_local), pl.ds(q * rows, rows)]

    def pair_part(slot, q):
        return buf.at[slot, pl.ds(occ_local, occ_local), pl.ds(q * rows, rows)]

    def to_right(slot, q, src=None):
        return pltpu.make_async_remote_copy(
            src_ref=own_part(slot, q) if src is None else src,
            dst_ref=own_part(slot + 1, q),
            send_sem=right_send.at[slot, q],
            recv_sem=right_recv.at[slot + 1, q],
            device_id={"vir": right},
            device_id_type=MESH,
        )

    def to_left(slot, q, src=None):
        return pltpu.make_async_remote_copy(
            src_ref=own_part(slot % n, q) if src is None else src,
            dst_ref=own_part(slot - 1, q),
            send_sem=left_send.at[n - slot, q],
            recv_sem=left_recv.at[n - slot + 1, q],
            device_id={"vir": left},
            device_id_type=MESH,
        )

    def to_pair(slot, q, src=None):
        return pltpu.make_async_remote_copy(
            src_ref=own_part(slot, q) if src is None else src,
            dst_ref=pair_part(slot, q),
            send_sem=pair_send.at[slot, q],
            recv_sem=pair_recv.at[slot, q],
            device_id={"occ": pair},
            device_id_type=MESH,
        )

    def x_part(q):
        return x_ref.at[:, pl.ds(q * rows, rows)]

    own_copy = pltpu.make_async_copy(x_ref, buf.at[0, pl.ds(0, occ_local)], local_sem)
    for q in range(chunks):
        to_right(0, q, x_part(q)).start()
        to_left(n, chunks - 1 - q, x_part(chunks - 1 - q)).start()
    own_copy.start()
    for q in range(chunks):
        to_pair(0, q, x_part(q)).start()
    out_ref[...] = jnp.zeros_like(out_ref)
    own_copy.wait()

    diagonal = lax.broadcasted_iota(jnp.int32, (vir_local, vir_local), 0) == (
        lax.broadcasted_iota(jnp.int32, (vir_local, vir_local), 1)
    )
    own_row = vir_ref[pl.ds(me, 1), :].astype(jnp.float32)
    own_column = jnp.sum(jnp.where(diagonal, own_row, 0.0), axis=1, keepdims=True)
    own_occ = [occ_ref[core * occ_local + i].astype(jnp.float32) for i in range(occ_local)]
    pair_occ = [occ_ref[pair * occ_local + i].astype(jnp.float32) for i in range(occ_local)]

    def compute(slot):
        source = at_place((place - slot + n) % n)
        energy_row = vir_ref[pl.ds(source, 1), :].astype(jnp.float32)
        base = own_column + energy_row
        amplitude = pair_amplitude(
            buf, 0, slot, base, own_occ, pair_occ, occ_local, vir_local, aux
        )

        step = 1024 if aux % 1024 == 0 else aux

        @pl.loop(0, aux // step)
        def _(t):
            columns = pl.ds(pl.multiple_of(t * step, step), step)
            there = buf[slot, :, :, columns].reshape(2 * occ_local * vir_local, step)
            part = jnp.dot(amplitude, there, preferred_element_type=jnp.float32)
            out_ref[:, :, columns] += part.reshape(occ_local, vir_local, step)

    def step_body(h, carry):
        @pl.when(h == 0)
        def _():
            for q in range(chunks):
                to_pair(0, q).wait_recv()

        @pl.when((h > 0) & (h < half))
        def _():
            for q in range(chunks):
                back = chunks - 1 - q
                to_right(h - 1, q).wait_recv()
                if q < chunks // 2:
                    to_right(h, q).start()
                else:
                    @pl.when(h < half - 1)
                    def _():
                        to_right(h, q).start()
                to_pair(h, q).start()
                to_left(n - h + 1, back).wait_recv()
                if back >= chunks // 2:
                    to_left(n - h, back).start()
                else:
                    @pl.when(h < half - 1)
                    def _():
                        to_left(n - h, back).start()
                to_pair(n - h, back).start()
            for q in range(chunks):
                to_pair(h, q).wait_recv()
                to_pair(n - h, chunks - 1 - q).wait_recv()

        @pl.when(h == half)
        def _():
            for q in range(chunks // 2):
                back = chunks - 1 - q
                to_right(half - 1, q).wait_recv()
                to_pair(half, q).start()
                to_left(half + 1, back).wait_recv()
                to_pair(half, back).start()
            for q in range(chunks):
                to_pair(half, q).wait_recv()

        both = jnp.where((h > 0) & (h < half), 2, 1)

        @pl.loop(0, both)
        def _(side):
            compute(h * (1 - side) + (n - h) * side)

        return carry

    lax.fori_loop(0, half + 1, step_body, 0)

    for h in range(half):
        for q in range(chunks):
            if h < half - 1 or q < chunks // 2:
                to_right(h, q).wait_send()
            if h < half - 1 or q >= chunks // 2:
                to_left(n - h, q, x_part(q) if h == 0 else None).wait_send()
    for slot in range(n):
        for q in range(chunks):
            to_pair(slot, q).wait_send()


def solution(mesh):
    n = mesh.shape["vir"]
    natural = ring_is_natural(mesh)
    grid = grid_of(mesh)

    def on_device(factors, occ_energy, vir_energy):
        occ_local, vir_local, aux = factors.shape
        dma = pltpu.SemaphoreType.DMA
        blocks = pltpu.VMEM((n, 2 * occ_local, vir_local, aux), jnp.bfloat16)
        parts, tiles = 8, 12
        fits = occ_local == 2 and vir_local == 128 and aux % (tiles * 128) == 0
        if grid and fits:
            chunks, wide = occ_local * parts, occ_local * vir_local
            early, lead = 5, 3
            body = functools.partial(grid_kernel, chunks // 2, early, lead)
            scratch = [
                blocks,
                pltpu.VMEM((occ_local, vir_local, aux), jnp.float32),
                pltpu.VMEM((tiles, occ_local, vir_local, aux // tiles), jnp.bfloat16),
                pltpu.VMEM((tiles, occ_local, vir_local, aux // tiles), jnp.bfloat16),
                pltpu.VMEM((wide, 2 * wide), jnp.bfloat16),
                pltpu.VMEM((2, 2, wide, wide), jnp.bfloat16),
                dma,
                *[dma((3, chunks))] * 2,
                *[dma((2, chunks))] * 2,
                *[dma((3, chunks))] * 2,
                *[dma((n, parts))] * 2,
                *[dma((tiles,))] * 2,
                *[dma((2, 2))] * 2,
            ]
        else:
            chunks = 4
            body = functools.partial(kernel, n, natural, chunks)
            scratch = [
                blocks,
                dma,
                *[dma((n // 2, chunks)), dma((n // 2 + 1, chunks))] * 2,
                *[dma((n, chunks))] * 2,
            ]
        return pl.pallas_call(
            body,
            out_shape=pltpu.VMEM((occ_local, vir_local, aux), jnp.float32),
            in_specs=[
                pl.BlockSpec(memory_space=pl.ANY),
                pl.BlockSpec(memory_space=pltpu.SMEM),
                pl.BlockSpec(memory_space=pltpu.VMEM),
            ],
            out_specs=pl.BlockSpec(memory_space=pltpu.VMEM),
            scratch_shapes=scratch,
            compiler_params=pltpu.CompilerParams(
                collective_id=0, has_side_effects=True, vmem_limit_bytes=56 * 1024 * 1024
            ),
            name="ring_density",
        )(pltpu.with_memory_space_constraint(factors, pltpu.HBM), occ_energy, vir_energy.reshape(n, vir_local))

    return jax.shard_map(
        on_device,
        mesh=mesh,
        in_specs=(P(("frag", "occ"), "vir", None), P("frag"), P("frag")),
        out_specs=P(("frag", "occ"), "vir", None),
        check_vma=False,
    )
```

```python
import functools

import jax
import jax.numpy as jnp
from jax import lax
from jax.experimental import pallas as pl
from jax.experimental.pallas import tpu as pltpu
from jax.sharding import PartitionSpec as P

MESH = pl.DeviceIdType.MESH
energy_unit = 1.0 / 1024.0
NT = (((1,), (1,)), ((), ()))


def ring_is_natural(mesh):
    axis = list(mesh.axis_names).index("vir")
    devices = mesh.devices.swapaxes(axis, -1)
    line = devices.reshape(-1, devices.shape[-1])[0]
    coords = [getattr(d, "coords", None) for d in line]
    if any(c is None for c in coords):
        return False
    return all(
        sum(abs(p - q) for p, q in zip(a, b)) <= 1 for a, b in zip(coords, coords[1:])
    )


def grid_of(mesh):
    axis = list(mesh.axis_names).index("vir")
    devices = mesh.devices.swapaxes(axis, -1)
    line = devices.reshape(-1, devices.shape[-1])[0]
    coords = [getattr(d, "coords", None) for d in line]
    if len(line) != 8 or any(c is None for c in coords):
        return False

    def near(a, b):
        return sum(abs(p - q) for p, q in zip(coords[a], coords[b])) == 1

    return all(near(k, k + 1) for k in range(0, 8, 2)) and all(near(k, k + 2) for k in range(6))


def pair_amplitude(buf, a_slot, b_slot, base, own_occ, pair_occ, occ_local, vir_local, aux):
    wide = occ_local * vir_local
    here_own = buf[a_slot, 0:occ_local].reshape(wide, aux)
    here_all = buf[a_slot].reshape(2 * wide, aux)
    there_own = buf[b_slot, 0:occ_local].reshape(wide, aux)
    there_pair = buf[b_slot, occ_local:].reshape(wide, aux)
    with_own = lax.dot_general(
        here_all, there_own, NT, preferred_element_type=jnp.float32
    ).astype(jnp.bfloat16).astype(jnp.float32)
    with_pair = lax.dot_general(
        here_own, there_pair, NT, preferred_element_type=jnp.float32
    ).astype(jnp.bfloat16).astype(jnp.float32)

    def block(values, i, j):
        return values[i * vir_local:(i + 1) * vir_local, j * vir_local:(j + 1) * vir_local]

    bands = []
    for i in range(occ_local):
        band = []
        for j in range(occ_local):
            divisor = ((own_occ[i] + own_occ[j]) - base) * energy_unit
            band.append((2.0 * block(with_own, i, j) - block(with_own, j, i)) / divisor)
        for j in range(occ_local):
            divisor = ((own_occ[i] + pair_occ[j]) - base) * energy_unit
            crossed = block(with_own, occ_local + j, i)
            band.append((2.0 * block(with_pair, i, j) - crossed) / divisor)
        bands.append(jnp.concatenate(band, axis=1))
    return jnp.concatenate(bands, axis=0).astype(jnp.bfloat16)


def half_amplitude(buf, a_slot, b_slot, h, a_column, b_row, own_occ, pair_occ, occ_local, vir_local,
                   aux):
    wide, half = occ_local * vir_local, vir_local // 2
    here_own = buf[a_slot, 0:occ_local].reshape(wide, aux)
    here_all = buf[a_slot].reshape(2 * wide, aux)
    rows = pl.ds(pl.multiple_of(h * half, half), half)
    there_own = buf[b_slot, 0:occ_local, rows].reshape(occ_local * half, aux)
    there_pair = buf[b_slot, occ_local:, rows].reshape(occ_local * half, aux)
    with_own = lax.dot_general(
        here_all, there_own, NT, preferred_element_type=jnp.float32
    ).astype(jnp.bfloat16).astype(jnp.float32)
    with_pair = lax.dot_general(
        here_own, there_pair, NT, preferred_element_type=jnp.float32
    ).astype(jnp.bfloat16).astype(jnp.float32)

    low = lax.broadcasted_iota(jnp.int32, (1, vir_local), 1) < half

    def swap(values):
        return pltpu.roll(values, half, 1)

    def band(k):
        return with_own[k * vir_local:(k + 1) * vir_local]

    turned = swap(b_row)
    first = jnp.where(h == 0, b_row, turned)
    second = jnp.where(h == 0, turned, b_row)
    base = a_column + jnp.where(low, first, second)
    own_row = jnp.where(low, own_occ[0], own_occ[1])
    pair_row = jnp.where(low, pair_occ[0], pair_occ[1])
    bands = []
    for i in range(2):
        if i == 0:
            crossed = jnp.where(low, band(0), swap(band(1)))
            crossed_pair = jnp.where(low, band(2), swap(band(3)))
        else:
            crossed = jnp.where(low, swap(band(0)), band(1))
            crossed_pair = jnp.where(low, swap(band(2)), band(3))
        direct_pair = with_pair[i * vir_local:(i + 1) * vir_local]
        divisor = ((own_occ[i] + own_row) - base) * energy_unit
        divisor_pair = ((own_occ[i] + pair_row) - base) * energy_unit
        bands.append(jnp.concatenate([
            (2.0 * band(i) - crossed) / divisor, (2.0 * direct_pair - crossed_pair) / divisor_pair
        ], axis=1))
    return jnp.concatenate(bands, axis=0).astype(jnp.bfloat16)


E0, E1, M0, M1, F0, F1, G0, G1 = range(8)


def pick(s, table, default=-1):
    value = default
    for step, entry in table.items():
        value = jnp.where(s == step, entry, value)
    return value


def grid_kernel(share, early, lead, x_ref, occ_ref, vir_ref, out_ref, buf, sum_acc, sum_out, sum_in, amp,
                given_amp, local_sem, row_send, row_recv, end_send, end_recv, mid_send, mid_recv,
                pair_send, pair_recv, sum_send, sum_recv, amp_send, amp_recv):
    occ_local, vir_local, aux = x_ref.shape
    parts = row_send.shape[1] // occ_local
    rows = vir_local // parts
    chunks = parts * occ_local
    tiles = sum_send.shape[0]
    step = aux // tiles
    half_parts = parts // 2
    half = vir_local // 2
    cuts = (aux, early[0] * step, early[1] * step)
    core = lax.axis_index("occ")
    me = lax.axis_index("vir")
    pair = 1 - core
    column, row = me // 2, me % 2
    side = column // 2
    is_mid = (column + side) % 2
    mid, end = is_mid == 1, is_mid == 0

    def name_to_vir(slot):
        at, flip = slot // 2, slot % 2
        column_at = (1 - side) * at + side * (3 - at)
        return 2 * column_at + row + flip - 2 * row * flip

    other_row = 2 * column + 1 - row
    along = 2 * (is_mid * (3 * side) + (1 - is_mid) * (1 + side)) + row
    across = 2 * (3 - column) + row

    barrier = pltpu.get_barrier_semaphore()
    for target in ({"vir": other_row}, {"vir": along}, {"occ": pair}):
        pl.semaphore_signal(barrier, inc=1, device_id=target, device_id_type=MESH)

    @pl.when(mid)
    def _():
        pl.semaphore_signal(barrier, inc=1, device_id={"vir": across}, device_id_type=MESH)

    pl.semaphore_wait(barrier, 3 + is_mid)

    def part(slot, c, few=0):
        where = (slot, c % occ_local, pl.ds((c // occ_local) * rows, rows))
        return buf.at[where + ((pl.ds(0, cuts[few]),) if few else ())]

    def x_part(c):
        return x_ref.at[c % occ_local, pl.ds((c // occ_local) * rows, rows)]

    def copy(src, dst, sends, recvs, order, c, target):
        return pltpu.make_async_remote_copy(
            src_ref=src, dst_ref=dst, send_sem=sends.at[order, c], recv_sem=recvs.at[order, c],
            device_id=target, device_id_type=MESH,
        )

    def to_row(order, slot, c, src=None, few=0):
        there = slot + 1 - 2 * (slot % 2)
        return copy(part(slot, c, few) if src is None else src, part(there, c, few),
                    row_send, row_recv, order, c, {"vir": other_row})

    def to_end(order, slot, c, src=None, few=0):
        return copy(part(slot, c, few) if src is None else src, part(slot, c, few),
                    end_send, end_recv, order, c, {"vir": along})

    def to_mid(order, slot, c, src=None):
        there = 6 - 2 * (slot // 2) + slot % 2
        return copy(part(slot, c) if src is None else src, part(there, c),
                    mid_send, mid_recv, order, c, {"vir": across})

    def to_pair(slot, q, few=0):
        tail = (pl.ds(q * rows, rows),) + ((pl.ds(0, cuts[few]),) if few else ())
        return copy(buf.at[(slot, pl.ds(0, occ_local)) + tail],
                    buf.at[(slot, pl.ds(occ_local, occ_local)) + tail],
                    pair_send, pair_recv, slot, q, {"occ": pair})

    def to_sum(t):
        return pltpu.make_async_remote_copy(
            src_ref=sum_out.at[t], dst_ref=sum_in.at[t], send_sem=sum_send.at[t],
            recv_sem=sum_recv.at[t], device_id={"vir": along}, device_id_type=MESH,
        )

    def to_amp(k, h):
        return copy(given_amp.at[k, h], given_amp.at[k, h], amp_send, amp_recv, k, h,
                    {"vir": along})

    own = is_mid * M0 + (1 - is_mid) * E0
    own_copy = pltpu.make_async_copy(x_ref, buf.at[own, pl.ds(0, occ_local)], local_sem)

    @pl.when(mid)
    def _():
        for c in range(lead):
            to_mid(1, M0, c, x_part(c)).start()

    @pl.loop(0, chunks)
    def _(c):
        @pl.when(end)
        def _():
            to_end(0, E0, c, x_part(c)).start()

        to_row(0, own, c, x_part(c)).start()

    own_copy.start()
    out_ref[...] = jnp.zeros_like(out_ref)

    @pl.when(mid)
    def _():
        sum_acc[...] = jnp.zeros_like(sum_acc)

    own_copy.wait()

    @pl.loop(0, parts)
    def _(q):
        to_pair(own, q).start()

    diagonal = lax.broadcasted_iota(jnp.int32, (vir_local, vir_local), 0) == (
        lax.broadcasted_iota(jnp.int32, (vir_local, vir_local), 1)
    )
    own_occ = [occ_ref[core * occ_local + i].astype(jnp.float32) for i in range(occ_local)]
    pair_occ = [occ_ref[pair * occ_local + i].astype(jnp.float32) for i in range(occ_local)]

    def energies(slot):
        return vir_ref[pl.ds(name_to_vir(slot), 1), :].astype(jnp.float32)

    def column_of(slot):
        return jnp.sum(jnp.where(diagonal, energies(slot), 0.0), axis=1, keepdims=True)

    def tile(t, width):
        return pl.ds(pl.multiple_of(t * width, width), width)

    def product(b_slot, columns):
        there = buf[b_slot, :, :, columns].reshape(2 * occ_local * vir_local, columns.size)
        piece = jnp.dot(amp[...], there, preferred_element_type=jnp.float32)
        return piece.reshape(occ_local, vir_local, columns.size)

    def half_product(k, h, columns):
        rows_h = pl.ds(pl.multiple_of(h * half, half), half)
        there = buf[F0 + k, :, rows_h, columns].reshape(2 * occ_local * half, columns.size)
        piece = jnp.dot(given_amp[k, h], there, preferred_element_type=jnp.float32)
        return piece.reshape(occ_local, vir_local, columns.size)

    def send_sum(t):
        columns = tile(t, step)
        sum_out[t] = sum_acc[:, :, columns].astype(jnp.bfloat16)
        to_sum(t).start()

    low_columns = [pl.ds(0, cut) for cut in cuts[1:]]
    high_columns = [pl.ds(cut, aux - cut) for cut in cuts[1:]]

    def arrive(role, s, first, count, body, order=None):
        @pl.when(role & (s >= first) & (s < first + count))
        def _():
            c = s - first
            body(c if order is None else order(c))

    def pair_on(slot, c, last=occ_local - 1, few=0):
        @pl.when(c % occ_local == last)
        def _():
            to_pair(slot, c // occ_local, few).start()

    def by_half(c, half_count, act):
        @pl.when(c < half_count)
        def _():
            act(1)

        @pl.when(c >= half_count)
        def _():
            act(2)

    half_chunks = chunks // 2
    turn = chunks + 2
    wait_far = max(lead, 2)
    close = 2 * chunks + 1
    last = close + 2 + chunks - share

    def mid_arrivals(s):
        def e0(c):
            to_end(0, E0, c).wait_recv()
            to_mid(0, E0, c).start()
            pair_on(E0, c)

        def g0(c):
            to_mid(0, E0, c).wait_recv()
            to_end(0, G0, c).start()
            pair_on(G0, c)

        def m1(c):
            to_row(0, M0, c).wait_recv()
            pair_on(M1, c)

        def own_rest(_):
            @pl.loop(lead, chunks)
            def _(c):
                to_mid(1, M0, c, x_part(c)).start()

        def f0(c):
            to_mid(1, M0, c).wait_recv()
            by_half(c, half_chunks, lambda few: to_end(1, F0, c, few=few).start())
            to_row(1, F0, c).start()
            pair_on(F0, c)

        def f1(c):
            to_row(1, F0, c).wait_recv()
            pair_on(F1, c)

        def g0_first(_):
            to_row(2, G0, share).start()

        def g0_row(_):
            @pl.loop(share + 1, chunks)
            def _(c):
                to_row(2, G0, c).start()

        def e1(c):
            to_end(1, E1, c).wait_recv()

            @pl.when(c < share)
            def _():
                to_mid(2, E1, c).start()

            pair_on(E1, c)

        def g1(c):
            to_row(2, G0, c).wait_recv()
            pair_on(G1, c)

        def g1_rest(_):
            @pl.loop(0, share)
            def _(c):
                to_mid(2, E1, c).wait_recv()
                pair_on(G1, c)

        arrive(mid, s, 0, chunks, e0)
        arrive(mid, s, chunks - 1, 1, own_rest)
        arrive(mid, s, 1, lead, f0)
        arrive(mid, s, wait_far, chunks, g0)
        arrive(mid, s, 1, chunks, m1)
        arrive(mid, s, turn - 1 + lead, chunks - lead, f0, lambda c: c + lead)
        arrive(mid, s, turn + 1, chunks, f1)
        arrive(mid, s, turn - 1, 1, g0_first)
        arrive(mid, s, close, 1, g0_row)
        arrive(mid, s, turn, chunks, e1)
        arrive(mid, s, close + 2, chunks - share, g1, lambda c: c + share)
        arrive(mid, s, last, 1, g1_rest)

    def end_arrivals(s):
        def e1(c):
            to_row(0, E0, c).wait_recv()
            to_end(1, E1, c).start()
            pair_on(E1, c)

        def g0(c):
            to_end(0, G0, c).wait_recv()
            to_row(1, G0, c).start()
            pair_on(G0, c)

        def f0(c):
            def act(few):
                to_end(1, F0, c, few=few).wait_recv()
                to_row(2, F0, c, few=few).start()
                pair_on(F0, c, few=few)

            by_half(c, half_chunks, act)

        def g1(c):
            to_row(1, G0, c).wait_recv()
            pair_on(G1, c)

        def f1(c):
            def act(few):
                to_row(2, F0, c, few=few).wait_recv()
                pair_on(F1, c, few=few)

            by_half(c, half_chunks, act)

        arrive(end, s, 1, chunks, e1)
        arrive(end, s, 3, lead, f0)
        arrive(end, s, wait_far + 2, chunks, g0)
        arrive(end, s, turn + 2 + lead, chunks - lead, f0, lambda c: c + lead)
        arrive(end, s, turn + 1, chunks, g1)
        arrive(end, s, turn + 9, chunks, f1)

    first_half, second_half = chunks // 2 - 1, chunks - 1
    mid_for_end = {chunks: M0, turn: M1}
    mid_half = {turn + first_half + 1: 0, turn + first_half + 3: 2, close: 1, close + 1: 3}
    mid_own = {turn + 3: M0, close + 2: E0, close + 3: M1, close + 4: G0, close + 5: F0, close + 6: F1, close + 7: E1, last: G1}
    end_own = {2: E0, turn: E1, turn + 3: G0, close + 3: G1}
    end_half = {close + 4: 0, close + 6: 2, close + 8: 1, close + 10: 3}
    steps = max(last + 1, close + 10) + 1

    def one(s, carry):
        mid_arrivals(s)
        end_arrivals(s)
        def jobs(at):
            return (is_mid * (pick(at, mid_for_end) + 1) - 1,
                    is_mid * pick(at, mid_own) + (1 - is_mid) * pick(at, end_own))

        code = is_mid * pick(s, mid_half) + (1 - is_mid) * pick(s, end_half)
        k, h = code // 2, code % 2
        for_end, for_own = jobs(s - 1)

        @pl.when(for_own >= 0)
        def _():
            out_ref[...] += product(for_own, pl.ds(0, aux))

        @pl.when(for_end >= 0)
        def _():
            sum_acc[:, :, low_columns[0]] += product(for_end, low_columns[0])

            @pl.when(for_end == M1)
            def _():
                @pl.loop(0, early[0])
                def _(t):
                    send_sum(t)

            sum_acc[:, :, high_columns[0]] += product(for_end, high_columns[0])

        next_for_end, next_for_own = jobs(s)
        b_slot = jnp.maximum(next_for_end, next_for_own)
        new = end | (next_for_end >= 0) | (b_slot == G0) | (b_slot == E1) | (b_slot == G1)

        @pl.when((b_slot >= 0) & new)
        def _():
            @pl.loop(0, parts)
            def _(q):
                to_pair(b_slot, q).wait_recv()

        @pl.when(mid & (s == chunks))
        def _():
            @pl.loop(0, parts)
            def _(q):
                to_pair(E0, q).wait_recv()

        @pl.when(b_slot >= 0)
        def _():
            a_slot = jnp.where(next_for_end >= 0, E0, own)
            base = column_of(a_slot) + energies(b_slot)
            amp[...] = pair_amplitude(
                buf, a_slot, b_slot, base, own_occ, pair_occ, occ_local, vir_local, aux
            )

        @pl.when(mid & (code >= 0))
        def _():
            @pl.loop(h * half_parts, (h + 1) * half_parts)
            def _(q):
                to_pair(F0 + k, q).wait_recv()

            given_amp[k, h] = half_amplitude(
                buf, E0, F0 + k, h, column_of(E0), energies(F0 + k), own_occ, pair_occ,
                occ_local, vir_local, aux,
            )
            to_amp(k, h).start()

            for level in range(2):
                @pl.when(h == level)
                def _():
                    sum_acc[:, :, high_columns[level]] += half_product(k, h, high_columns[level])

            @pl.when(k == 1)
            def _():
                @pl.loop(jnp.where(h == 0, early[0], early[1]), jnp.where(h == 0, early[1], tiles))
                def _(t):
                    send_sum(t)

        @pl.when(end & (code >= 0))
        def _():
            to_amp(k, h).wait_recv()

            for level in range(2):
                @pl.when(h == level)
                def _():
                    @pl.loop(level * half_parts, (level + 1) * half_parts)
                    def _(q):
                        to_pair(F0 + k, q, few=level + 1).wait_recv()

                    out_ref[:, :, low_columns[level]] += half_product(k, h, low_columns[level])

        return carry

    lax.fori_loop(0, steps, one, 0)

    @pl.when(end)
    def _():
        @pl.loop(0, tiles)
        def _(t):
            columns = tile(t, step)
            to_sum(t).wait_recv()
            out_ref[:, :, columns] += sum_in[t].astype(jnp.float32)

    @pl.loop(0, chunks)
    def _(c):
        to_row(0, own, c, x_part(c)).wait_send()
        to_row(1, F0, c).wait_send()
        to_end(0, E0, c).wait_send()

        @pl.when(mid)
        def _():
            by_half(c, half_chunks, lambda few: to_end(1, F0, c, few=few).wait_send())
            to_mid(0, E0, c).wait_send()
            to_mid(1, M0, c, x_part(c)).wait_send()

            @pl.when(c >= share)
            def _():
                to_row(2, G0, c).wait_send()

            @pl.when(c < share)
            def _():
                to_mid(2, E1, c).wait_send()

        @pl.when(end)
        def _():
            to_end(1, E1, c).wait_send()
            by_half(c, half_chunks, lambda few: to_row(2, F0, c, few=few).wait_send())

    @pl.loop(0, parts)
    def _(q):
        for slot in (E0, E1, G0, G1):
            to_pair(slot, q).wait_send()

        for slot in (M0, M1):
            @pl.when(mid)
            def _():
                to_pair(slot, q).wait_send()

        for slot in (F0, F1):
            @pl.when(mid)
            def _():
                to_pair(slot, q).wait_send()

            @pl.when(end)
            def _():
                by_half(q, half_parts, lambda few: to_pair(slot, q, few=few).wait_send())

    @pl.when(mid)
    def _():
        for k in range(2):
            for h in range(2):
                to_amp(k, h).wait_send()

        @pl.loop(0, tiles)
        def _(t):
            to_sum(t).wait_send()


def kernel(n, natural, chunks, x_ref, occ_ref, vir_ref, out_ref, buf, local_sem,
           right_send, right_recv, left_send, left_recv, pair_send, pair_recv):
    occ_local, vir_local, aux = x_ref.shape
    half = n // 2
    rows = vir_local // chunks
    core = lax.axis_index("occ")
    me = lax.axis_index("vir")

    if natural:
        place = me

        def at_place(k):
            return k
    else:
        odd = me % 2
        place = (1 - odd) * (me // 2) + odd * (n - 1 - me // 2)

        def at_place(k):
            down = k // half
            return (1 - down) * (2 * k) + down * (2 * (n - k) - 1)

    right = at_place((place + 1) % n)
    left = at_place((place + n - 1) % n)
    pair = 1 - core

    barrier = pltpu.get_barrier_semaphore()
    for target in ({"vir": right}, {"vir": left}, {"occ": pair}):
        pl.semaphore_signal(barrier, inc=1, device_id=target, device_id_type=MESH)
    pl.semaphore_wait(barrier, 3)

    def own_part(slot, q):
        return buf.at[slot, pl.ds(0, occ_local), pl.ds(q * rows, rows)]

    def pair_part(slot, q):
        return buf.at[slot, pl.ds(occ_local, occ_local), pl.ds(q * rows, rows)]

    def to_right(slot, q, src=None):
        return pltpu.make_async_remote_copy(
            src_ref=own_part(slot, q) if src is None else src,
            dst_ref=own_part(slot + 1, q),
            send_sem=right_send.at[slot, q],
            recv_sem=right_recv.at[slot + 1, q],
            device_id={"vir": right},
            device_id_type=MESH,
        )

    def to_left(slot, q, src=None):
        return pltpu.make_async_remote_copy(
            src_ref=own_part(slot % n, q) if src is None else src,
            dst_ref=own_part(slot - 1, q),
            send_sem=left_send.at[n - slot, q],
            recv_sem=left_recv.at[n - slot + 1, q],
            device_id={"vir": left},
            device_id_type=MESH,
        )

    def to_pair(slot, q, src=None):
        return pltpu.make_async_remote_copy(
            src_ref=own_part(slot, q) if src is None else src,
            dst_ref=pair_part(slot, q),
            send_sem=pair_send.at[slot, q],
            recv_sem=pair_recv.at[slot, q],
            device_id={"occ": pair},
            device_id_type=MESH,
        )

    def x_part(q):
        return x_ref.at[:, pl.ds(q * rows, rows)]

    own_copy = pltpu.make_async_copy(x_ref, buf.at[0, pl.ds(0, occ_local)], local_sem)
    for q in range(chunks):
        to_right(0, q, x_part(q)).start()
        to_left(n, chunks - 1 - q, x_part(chunks - 1 - q)).start()
    own_copy.start()
    for q in range(chunks):
        to_pair(0, q, x_part(q)).start()
    out_ref[...] = jnp.zeros_like(out_ref)
    own_copy.wait()

    diagonal = lax.broadcasted_iota(jnp.int32, (vir_local, vir_local), 0) == (
        lax.broadcasted_iota(jnp.int32, (vir_local, vir_local), 1)
    )
    own_row = vir_ref[pl.ds(me, 1), :].astype(jnp.float32)
    own_column = jnp.sum(jnp.where(diagonal, own_row, 0.0), axis=1, keepdims=True)
    own_occ = [occ_ref[core * occ_local + i].astype(jnp.float32) for i in range(occ_local)]
    pair_occ = [occ_ref[pair * occ_local + i].astype(jnp.float32) for i in range(occ_local)]

    def compute(slot):
        source = at_place((place - slot + n) % n)
        energy_row = vir_ref[pl.ds(source, 1), :].astype(jnp.float32)
        base = own_column + energy_row
        amplitude = pair_amplitude(
            buf, 0, slot, base, own_occ, pair_occ, occ_local, vir_local, aux
        )

        step = 1024 if aux % 1024 == 0 else aux

        @pl.loop(0, aux // step)
        def _(t):
            columns = pl.ds(pl.multiple_of(t * step, step), step)
            there = buf[slot, :, :, columns].reshape(2 * occ_local * vir_local, step)
            part = jnp.dot(amplitude, there, preferred_element_type=jnp.float32)
            out_ref[:, :, columns] += part.reshape(occ_local, vir_local, step)

    def step_body(h, carry):
        @pl.when(h == 0)
        def _():
            for q in range(chunks):
                to_pair(0, q).wait_recv()

        @pl.when((h > 0) & (h < half))
        def _():
            for q in range(chunks):
                back = chunks - 1 - q
                to_right(h - 1, q).wait_recv()
                if q < chunks // 2:
                    to_right(h, q).start()
                else:
                    @pl.when(h < half - 1)
                    def _():
                        to_right(h, q).start()
                to_pair(h, q).start()
                to_left(n - h + 1, back).wait_recv()
                if back >= chunks // 2:
                    to_left(n - h, back).start()
                else:
                    @pl.when(h < half - 1)
                    def _():
                        to_left(n - h, back).start()
                to_pair(n - h, back).start()
            for q in range(chunks):
                to_pair(h, q).wait_recv()
                to_pair(n - h, chunks - 1 - q).wait_recv()

        @pl.when(h == half)
        def _():
            for q in range(chunks // 2):
                back = chunks - 1 - q
                to_right(half - 1, q).wait_recv()
                to_pair(half, q).start()
                to_left(half + 1, back).wait_recv()
                to_pair(half, back).start()
            for q in range(chunks):
                to_pair(half, q).wait_recv()

        both = jnp.where((h > 0) & (h < half), 2, 1)

        @pl.loop(0, both)
        def _(side):
            compute(h * (1 - side) + (n - h) * side)

        return carry

    lax.fori_loop(0, half + 1, step_body, 0)

    for h in range(half):
        for q in range(chunks):
            if h < half - 1 or q < chunks // 2:
                to_right(h, q).wait_send()
            if h < half - 1 or q >= chunks // 2:
                to_left(n - h, q, x_part(q) if h == 0 else None).wait_send()
    for slot in range(n):
        for q in range(chunks):
            to_pair(slot, q).wait_send()


def solution(mesh):
    n = mesh.shape["vir"]
    natural = ring_is_natural(mesh)
    grid = grid_of(mesh)

    def on_device(factors, occ_energy, vir_energy):
        occ_local, vir_local, aux = factors.shape
        dma = pltpu.SemaphoreType.DMA
        blocks = pltpu.VMEM((n, 2 * occ_local, vir_local, aux), jnp.bfloat16)
        parts, tiles = 8, 12
        fits = occ_local == 2 and vir_local == 128 and aux % (tiles * 128) == 0
        if grid and fits:
            chunks, wide = occ_local * parts, occ_local * vir_local
            early, lead = (4, 5), 3
            body = functools.partial(grid_kernel, chunks // 2, early, lead)
            scratch = [
                blocks,
                pltpu.VMEM((occ_local, vir_local, aux), jnp.float32),
                pltpu.VMEM((tiles, occ_local, vir_local, aux // tiles), jnp.bfloat16),
                pltpu.VMEM((tiles, occ_local, vir_local, aux // tiles), jnp.bfloat16),
                pltpu.VMEM((wide, 2 * wide), jnp.bfloat16),
                pltpu.VMEM((2, 2, wide, wide), jnp.bfloat16),
                dma,
                *[dma((3, chunks))] * 2,
                *[dma((2, chunks))] * 2,
                *[dma((3, chunks))] * 2,
                *[dma((n, parts))] * 2,
                *[dma((tiles,))] * 2,
                *[dma((2, 2))] * 2,
            ]
        else:
            chunks = 4
            body = functools.partial(kernel, n, natural, chunks)
            scratch = [
                blocks,
                dma,
                *[dma((n // 2, chunks)), dma((n // 2 + 1, chunks))] * 2,
                *[dma((n, chunks))] * 2,
            ]
        return pl.pallas_call(
            body,
            out_shape=pltpu.VMEM((occ_local, vir_local, aux), jnp.float32),
            in_specs=[
                pl.BlockSpec(memory_space=pl.ANY),
                pl.BlockSpec(memory_space=pltpu.SMEM),
                pl.BlockSpec(memory_space=pltpu.VMEM),
            ],
            out_specs=pl.BlockSpec(memory_space=pltpu.VMEM),
            scratch_shapes=scratch,
            compiler_params=pltpu.CompilerParams(
                collective_id=0, has_side_effects=True, vmem_limit_bytes=56 * 1024 * 1024
            ),
            name="ring_density",
        )(pltpu.with_memory_space_constraint(factors, pltpu.HBM), occ_energy, vir_energy.reshape(n, vir_local))

    return jax.shard_map(
        on_device,
        mesh=mesh,
        in_specs=(P(("frag", "occ"), "vir", None), P("frag"), P("frag")),
        out_specs=P(("frag", "occ"), "vir", None),
        check_vma=False,
    )
```

```python
import functools

import jax
import jax.numpy as jnp
from jax import lax
from jax.experimental import pallas as pl
from jax.experimental.pallas import tpu as pltpu
from jax.sharding import PartitionSpec as P

MESH = pl.DeviceIdType.MESH
energy_unit = 1.0 / 1024.0
NT = (((1,), (1,)), ((), ()))


def ring_is_natural(mesh):
    axis = list(mesh.axis_names).index("vir")
    devices = mesh.devices.swapaxes(axis, -1)
    line = devices.reshape(-1, devices.shape[-1])[0]
    coords = [getattr(d, "coords", None) for d in line]
    if any(c is None for c in coords):
        return False
    return all(
        sum(abs(p - q) for p, q in zip(a, b)) <= 1 for a, b in zip(coords, coords[1:])
    )


def grid_of(mesh):
    axis = list(mesh.axis_names).index("vir")
    devices = mesh.devices.swapaxes(axis, -1)
    line = devices.reshape(-1, devices.shape[-1])[0]
    coords = [getattr(d, "coords", None) for d in line]
    if len(line) != 8 or any(c is None for c in coords):
        return False

    def near(a, b):
        return sum(abs(p - q) for p, q in zip(coords[a], coords[b])) == 1

    return all(near(k, k + 1) for k in range(0, 8, 2)) and all(near(k, k + 2) for k in range(6))


def pair_amplitude(buf, a_slot, b_slot, base, own_occ, pair_occ, occ_local, vir_local, aux):
    wide = occ_local * vir_local
    here_own = buf[a_slot, 0:occ_local].reshape(wide, aux)
    here_all = buf[a_slot].reshape(2 * wide, aux)
    there_own = buf[b_slot, 0:occ_local].reshape(wide, aux)
    there_pair = buf[b_slot, occ_local:].reshape(wide, aux)
    with_own = lax.dot_general(
        here_all, there_own, NT, preferred_element_type=jnp.float32
    ).astype(jnp.bfloat16).astype(jnp.float32)
    with_pair = lax.dot_general(
        here_own, there_pair, NT, preferred_element_type=jnp.float32
    ).astype(jnp.bfloat16).astype(jnp.float32)

    def block(values, i, j):
        return values[i * vir_local:(i + 1) * vir_local, j * vir_local:(j + 1) * vir_local]

    bands = []
    for i in range(occ_local):
        band = []
        for j in range(occ_local):
            divisor = ((own_occ[i] + own_occ[j]) - base) * energy_unit
            band.append((2.0 * block(with_own, i, j) - block(with_own, j, i)) / divisor)
        for j in range(occ_local):
            divisor = ((own_occ[i] + pair_occ[j]) - base) * energy_unit
            crossed = block(with_own, occ_local + j, i)
            band.append((2.0 * block(with_pair, i, j) - crossed) / divisor)
        bands.append(jnp.concatenate(band, axis=1))
    return jnp.concatenate(bands, axis=0).astype(jnp.bfloat16)


def half_amplitude(buf, a_slot, b_slot, h, a_column, b_row, own_occ, pair_occ, occ_local, vir_local,
                   aux):
    wide, half = occ_local * vir_local, vir_local // 2
    here_own = buf[a_slot, 0:occ_local].reshape(wide, aux)
    here_all = buf[a_slot].reshape(2 * wide, aux)
    rows = pl.ds(pl.multiple_of(h * half, half), half)
    there_own = buf[b_slot, 0:occ_local, rows].reshape(occ_local * half, aux)
    there_pair = buf[b_slot, occ_local:, rows].reshape(occ_local * half, aux)
    with_own = lax.dot_general(
        here_all, there_own, NT, preferred_element_type=jnp.float32
    ).astype(jnp.bfloat16).astype(jnp.float32)
    with_pair = lax.dot_general(
        here_own, there_pair, NT, preferred_element_type=jnp.float32
    ).astype(jnp.bfloat16).astype(jnp.float32)

    low = lax.broadcasted_iota(jnp.int32, (1, vir_local), 1) < half

    def swap(values):
        return pltpu.roll(values, half, 1)

    def band(k):
        return with_own[k * vir_local:(k + 1) * vir_local]

    turned = swap(b_row)
    first = jnp.where(h == 0, b_row, turned)
    second = jnp.where(h == 0, turned, b_row)
    base = a_column + jnp.where(low, first, second)
    own_row = jnp.where(low, own_occ[0], own_occ[1])
    pair_row = jnp.where(low, pair_occ[0], pair_occ[1])
    bands = []
    for i in range(2):
        if i == 0:
            crossed = jnp.where(low, band(0), swap(band(1)))
            crossed_pair = jnp.where(low, band(2), swap(band(3)))
        else:
            crossed = jnp.where(low, swap(band(0)), band(1))
            crossed_pair = jnp.where(low, swap(band(2)), band(3))
        direct_pair = with_pair[i * vir_local:(i + 1) * vir_local]
        divisor = ((own_occ[i] + own_row) - base) * energy_unit
        divisor_pair = ((own_occ[i] + pair_row) - base) * energy_unit
        bands.append(jnp.concatenate([
            (2.0 * band(i) - crossed) / divisor, (2.0 * direct_pair - crossed_pair) / divisor_pair
        ], axis=1))
    return jnp.concatenate(bands, axis=0).astype(jnp.bfloat16)


E0, E1, M0, M1, F0, F1, G0, G1 = range(8)


def pick(s, table, default=-1):
    value = default
    for step, entry in table.items():
        value = jnp.where(s == step, entry, value)
    return value


def grid_kernel(share, early, lead, x_ref, occ_ref, vir_ref, out_ref, buf, sum_acc, sum_out, sum_in, amp,
                given_amp, local_sem, row_send, row_recv, end_send, end_recv, mid_send, mid_recv,
                pair_send, pair_recv, sum_send, sum_recv, amp_send, amp_recv):
    occ_local, vir_local, aux = x_ref.shape
    parts = row_send.shape[1] // occ_local
    rows = vir_local // parts
    chunks = parts * occ_local
    tiles = sum_send.shape[0]
    step = aux // tiles
    half_parts = parts // 2
    half = vir_local // 2
    cuts = (aux, early[0] * step, early[1] * step)
    core = lax.axis_index("occ")
    me = lax.axis_index("vir")
    pair = 1 - core
    column, row = me // 2, me % 2
    side = column // 2
    is_mid = (column + side) % 2
    mid, end = is_mid == 1, is_mid == 0

    def name_to_vir(slot):
        at, flip = slot // 2, slot % 2
        column_at = (1 - side) * at + side * (3 - at)
        return 2 * column_at + row + flip - 2 * row * flip

    other_row = 2 * column + 1 - row
    along = 2 * (is_mid * (3 * side) + (1 - is_mid) * (1 + side)) + row
    across = 2 * (3 - column) + row

    barrier = pltpu.get_barrier_semaphore()
    for target in ({"vir": other_row}, {"vir": along}, {"occ": pair}):
        pl.semaphore_signal(barrier, inc=1, device_id=target, device_id_type=MESH)

    @pl.when(mid)
    def _():
        pl.semaphore_signal(barrier, inc=1, device_id={"vir": across}, device_id_type=MESH)

    pl.semaphore_wait(barrier, 3 + is_mid)

    def part(slot, c, few=0):
        where = (slot, c % occ_local, pl.ds((c // occ_local) * rows, rows))
        return buf.at[where + ((pl.ds(0, cuts[few]),) if few else ())]

    def x_part(c):
        return x_ref.at[c % occ_local, pl.ds((c // occ_local) * rows, rows)]

    def copy(src, dst, sends, recvs, order, c, target):
        return pltpu.make_async_remote_copy(
            src_ref=src, dst_ref=dst, send_sem=sends.at[order, c], recv_sem=recvs.at[order, c],
            device_id=target, device_id_type=MESH,
        )

    def to_row(order, slot, c, src=None, few=0):
        there = slot + 1 - 2 * (slot % 2)
        return copy(part(slot, c, few) if src is None else src, part(there, c, few),
                    row_send, row_recv, order, c, {"vir": other_row})

    def to_end(order, slot, c, src=None, few=0):
        return copy(part(slot, c, few) if src is None else src, part(slot, c, few),
                    end_send, end_recv, order, c, {"vir": along})

    def to_mid(order, slot, c, src=None):
        there = 6 - 2 * (slot // 2) + slot % 2
        return copy(part(slot, c) if src is None else src, part(there, c),
                    mid_send, mid_recv, order, c, {"vir": across})

    def to_pair(slot, q, few=0):
        tail = (pl.ds(q * rows, rows),) + ((pl.ds(0, cuts[few]),) if few else ())
        return copy(buf.at[(slot, pl.ds(0, occ_local)) + tail],
                    buf.at[(slot, pl.ds(occ_local, occ_local)) + tail],
                    pair_send, pair_recv, slot, q, {"occ": pair})

    def to_sum(t):
        return pltpu.make_async_remote_copy(
            src_ref=sum_out.at[t], dst_ref=sum_in.at[t], send_sem=sum_send.at[t],
            recv_sem=sum_recv.at[t], device_id={"vir": along}, device_id_type=MESH,
        )

    def to_amp(k, h):
        return copy(given_amp.at[k, h], given_amp.at[k, h], amp_send, amp_recv, k, h,
                    {"vir": along})

    own = is_mid * M0 + (1 - is_mid) * E0
    own_copy = pltpu.make_async_copy(x_ref, buf.at[own, pl.ds(0, occ_local)], local_sem)

    @pl.when(mid)
    def _():
        for c in range(lead):
            to_mid(1, M0, c, x_part(c)).start()

    @pl.loop(0, chunks)
    def _(c):
        @pl.when(end)
        def _():
            to_end(0, E0, c, x_part(c)).start()

        to_row(0, own, c, x_part(c)).start()

    own_copy.start()
    out_ref[...] = jnp.zeros_like(out_ref)

    @pl.when(mid)
    def _():
        sum_acc[...] = jnp.zeros_like(sum_acc)

    own_copy.wait()

    @pl.loop(0, parts)
    def _(q):
        to_pair(own, q).start()

    diagonal = lax.broadcasted_iota(jnp.int32, (vir_local, vir_local), 0) == (
        lax.broadcasted_iota(jnp.int32, (vir_local, vir_local), 1)
    )
    own_occ = [occ_ref[core * occ_local + i].astype(jnp.float32) for i in range(occ_local)]
    pair_occ = [occ_ref[pair * occ_local + i].astype(jnp.float32) for i in range(occ_local)]

    def energies(slot):
        return vir_ref[pl.ds(name_to_vir(slot), 1), :].astype(jnp.float32)

    def column_of(slot):
        return jnp.sum(jnp.where(diagonal, energies(slot), 0.0), axis=1, keepdims=True)

    def tile(t, width):
        return pl.ds(pl.multiple_of(t * width, width), width)

    def product(b_slot, columns):
        there = buf[b_slot, :, :, columns].reshape(2 * occ_local * vir_local, columns.size)
        piece = jnp.dot(amp[...], there, preferred_element_type=jnp.float32)
        return piece.reshape(occ_local, vir_local, columns.size)

    def half_product(k, h, columns):
        rows_h = pl.ds(pl.multiple_of(h * half, half), half)
        there = buf[F0 + k, :, rows_h, columns].reshape(2 * occ_local * half, columns.size)
        piece = jnp.dot(given_amp[k, h], there, preferred_element_type=jnp.float32)
        return piece.reshape(occ_local, vir_local, columns.size)

    def send_sum(t):
        columns = tile(t, step)
        sum_out[t] = sum_acc[:, :, columns].astype(jnp.bfloat16)
        to_sum(t).start()

    low_columns = [pl.ds(0, cut) for cut in cuts[1:]]
    high_columns = [pl.ds(cut, aux - cut) for cut in cuts[1:]]

    def arrive(role, s, first, count, body, order=None):
        @pl.when(role & (s >= first) & (s < first + count))
        def _():
            c = s - first
            body(c if order is None else order(c))

    def pair_on(slot, c, last=occ_local - 1, few=0):
        @pl.when(c % occ_local == last)
        def _():
            to_pair(slot, c // occ_local, few).start()

    def by_half(c, half_count, act):
        @pl.when(c < half_count)
        def _():
            act(1)

        @pl.when(c >= half_count)
        def _():
            act(2)

    half_chunks = chunks // 2
    turn = chunks + 2
    wait_far = max(lead, 2)
    close = 2 * chunks + 1
    last = close + 2 + chunks - share

    def mid_arrivals(s):
        def e0(c):
            to_end(0, E0, c).wait_recv()
            to_mid(0, E0, c).start()
            pair_on(E0, c)

        def g0(c):
            to_mid(0, E0, c).wait_recv()
            to_end(0, G0, c).start()
            pair_on(G0, c)

        def m1(c):
            to_row(0, M0, c).wait_recv()

            @pl.when(c == chunks - 1)
            def _():
                to_mid(2, M1, c).start()

            pair_on(M1, c)

        def own_rest(_):
            @pl.loop(lead, chunks)
            def _(c):
                to_mid(1, M0, c, x_part(c)).start()

        def f0(c):
            to_mid(1, M0, c).wait_recv()
            by_half(c, half_chunks, lambda few: to_end(1, F0, c, few=few).start())

            @pl.when(c < chunks - 1)
            def _():
                to_row(1, F0, c).start()

            pair_on(F0, c)

        def f1(c):
            @pl.when(c < chunks - 1)
            def _():
                to_row(1, F0, c).wait_recv()

            @pl.when(c == chunks - 1)
            def _():
                to_mid(2, M1, c).wait_recv()

            pair_on(F1, c)

        def g0_first(_):
            to_row(2, G0, share).start()

        def g0_row(_):
            @pl.loop(share + 1, chunks)
            def _(c):
                to_row(2, G0, c).start()

        def e1(c):
            to_end(1, E1, c).wait_recv()

            @pl.when(c < share)
            def _():
                to_mid(2, E1, c).start()

            pair_on(E1, c)

        def g1(c):
            to_row(2, G0, c).wait_recv()
            pair_on(G1, c)

        def g1_rest(_):
            @pl.loop(0, share)
            def _(c):
                to_mid(2, E1, c).wait_recv()
                pair_on(G1, c)

        arrive(mid, s, 0, chunks, e0)
        arrive(mid, s, chunks - 1, 1, own_rest)
        arrive(mid, s, 1, lead, f0)
        arrive(mid, s, wait_far, chunks, g0)
        arrive(mid, s, 1, chunks, m1)
        arrive(mid, s, turn - 1 + lead, chunks - lead, f0, lambda c: c + lead)
        arrive(mid, s, turn + 1, chunks, f1)
        arrive(mid, s, turn - 1, 1, g0_first)
        arrive(mid, s, close, 1, g0_row)
        arrive(mid, s, turn, chunks, e1)
        arrive(mid, s, close + 2, chunks - share, g1, lambda c: c + share)
        arrive(mid, s, last, 1, g1_rest)

    def end_arrivals(s):
        def e1(c):
            to_row(0, E0, c).wait_recv()
            to_end(1, E1, c).start()
            pair_on(E1, c)

        def g0(c):
            to_end(0, G0, c).wait_recv()
            to_row(1, G0, c).start()
            pair_on(G0, c)

        def f0(c):
            def act(few):
                to_end(1, F0, c, few=few).wait_recv()
                to_row(2, F0, c, few=few).start()
                pair_on(F0, c, few=few)

            by_half(c, half_chunks, act)

        def g1(c):
            to_row(1, G0, c).wait_recv()
            pair_on(G1, c)

        def f1(c):
            def act(few):
                to_row(2, F0, c, few=few).wait_recv()
                pair_on(F1, c, few=few)

            by_half(c, half_chunks, act)

        arrive(end, s, 1, chunks, e1)
        arrive(end, s, 3, lead, f0)
        arrive(end, s, wait_far + 2, chunks, g0)
        arrive(end, s, turn + 2 + lead, chunks - lead, f0, lambda c: c + lead)
        arrive(end, s, turn + 1, chunks, g1)
        arrive(end, s, turn + 9, chunks, f1)

    first_half, second_half = chunks // 2 - 1, chunks - 1
    mid_for_end = {chunks: M0, turn: M1}
    mid_half = {turn + first_half + 1: 0, turn + first_half + 3: 2, close: 1, close + 1: 3}
    mid_own = {turn + 3: M0, close + 2: E0, close + 3: M1, close + 4: G0, close + 5: F0, close + 6: F1, close + 7: E1, last: G1}
    end_own = {2: E0, turn: E1, turn + 3: G0, close + 3: G1}
    end_half = {close + 4: 0, close + 6: 2, close + 8: 1, close + 10: 3}
    steps = max(last + 1, close + 10) + 1

    def one(s, carry):
        mid_arrivals(s)
        end_arrivals(s)
        def jobs(at):
            return (is_mid * (pick(at, mid_for_end) + 1) - 1,
                    is_mid * pick(at, mid_own) + (1 - is_mid) * pick(at, end_own))

        code = is_mid * pick(s, mid_half) + (1 - is_mid) * pick(s, end_half)
        k, h = code // 2, code % 2
        for_end, for_own = jobs(s - 1)

        @pl.when(for_own >= 0)
        def _():
            out_ref[...] += product(for_own, pl.ds(0, aux))

        @pl.when(for_end >= 0)
        def _():
            sum_acc[:, :, low_columns[0]] += product(for_end, low_columns[0])

            @pl.when(for_end == M1)
            def _():
                @pl.loop(0, early[0])
                def _(t):
                    send_sum(t)

            sum_acc[:, :, high_columns[0]] += product(for_end, high_columns[0])

        next_for_end, next_for_own = jobs(s)
        b_slot = jnp.maximum(next_for_end, next_for_own)
        new = end | (next_for_end >= 0) | (b_slot == G0) | (b_slot == E1) | (b_slot == G1)

        @pl.when((b_slot >= 0) & new)
        def _():
            @pl.loop(0, parts)
            def _(q):
                to_pair(b_slot, q).wait_recv()

        @pl.when(mid & (s == chunks))
        def _():
            @pl.loop(0, parts)
            def _(q):
                to_pair(E0, q).wait_recv()

        @pl.when(b_slot >= 0)
        def _():
            a_slot = jnp.where(next_for_end >= 0, E0, own)
            base = column_of(a_slot) + energies(b_slot)
            amp[...] = pair_amplitude(
                buf, a_slot, b_slot, base, own_occ, pair_occ, occ_local, vir_local, aux
            )

        @pl.when(mid & (code >= 0))
        def _():
            @pl.loop(h * half_parts, (h + 1) * half_parts)
            def _(q):
                to_pair(F0 + k, q).wait_recv()

            given_amp[k, h] = half_amplitude(
                buf, E0, F0 + k, h, column_of(E0), energies(F0 + k), own_occ, pair_occ,
                occ_local, vir_local, aux,
            )
            to_amp(k, h).start()

            for level in range(2):
                @pl.when(h == level)
                def _():
                    sum_acc[:, :, high_columns[level]] += half_product(k, h, high_columns[level])

            @pl.when(k == 1)
            def _():
                @pl.loop(jnp.where(h == 0, early[0], early[1]), jnp.where(h == 0, early[1], tiles))
                def _(t):
                    send_sum(t)

        @pl.when(end & (code >= 0))
        def _():
            to_amp(k, h).wait_recv()

            for level in range(2):
                @pl.when(h == level)
                def _():
                    @pl.loop(level * half_parts, (level + 1) * half_parts)
                    def _(q):
                        to_pair(F0 + k, q, few=level + 1).wait_recv()

                    out_ref[:, :, low_columns[level]] += half_product(k, h, low_columns[level])

        return carry

    lax.fori_loop(0, steps, one, 0)

    @pl.when(end)
    def _():
        @pl.loop(0, tiles)
        def _(t):
            columns = tile(t, step)
            to_sum(t).wait_recv()
            out_ref[:, :, columns] += sum_in[t].astype(jnp.float32)

    @pl.loop(0, chunks)
    def _(c):
        to_row(0, own, c, x_part(c)).wait_send()

        @pl.when(end | (c < chunks - 1))
        def _():
            to_row(1, F0, c).wait_send()

        to_end(0, E0, c).wait_send()

        @pl.when(mid)
        def _():
            by_half(c, half_chunks, lambda few: to_end(1, F0, c, few=few).wait_send())
            to_mid(0, E0, c).wait_send()
            to_mid(1, M0, c, x_part(c)).wait_send()

            @pl.when(c >= share)
            def _():
                to_row(2, G0, c).wait_send()

            @pl.when(c < share)
            def _():
                to_mid(2, E1, c).wait_send()

            @pl.when(c == chunks - 1)
            def _():
                to_mid(2, M1, c).wait_send()

        @pl.when(end)
        def _():
            to_end(1, E1, c).wait_send()
            by_half(c, half_chunks, lambda few: to_row(2, F0, c, few=few).wait_send())

    @pl.loop(0, parts)
    def _(q):
        for slot in (E0, E1, G0, G1):
            to_pair(slot, q).wait_send()

        for slot in (M0, M1):
            @pl.when(mid)
            def _():
                to_pair(slot, q).wait_send()

        for slot in (F0, F1):
            @pl.when(mid)
            def _():
                to_pair(slot, q).wait_send()

            @pl.when(end)
            def _():
                by_half(q, half_parts, lambda few: to_pair(slot, q, few=few).wait_send())

    @pl.when(mid)
    def _():
        for k in range(2):
            for h in range(2):
                to_amp(k, h).wait_send()

        @pl.loop(0, tiles)
        def _(t):
            to_sum(t).wait_send()


def kernel(n, natural, chunks, x_ref, occ_ref, vir_ref, out_ref, buf, local_sem,
           right_send, right_recv, left_send, left_recv, pair_send, pair_recv):
    occ_local, vir_local, aux = x_ref.shape
    half = n // 2
    rows = vir_local // chunks
    core = lax.axis_index("occ")
    me = lax.axis_index("vir")

    if natural:
        place = me

        def at_place(k):
            return k
    else:
        odd = me % 2
        place = (1 - odd) * (me // 2) + odd * (n - 1 - me // 2)

        def at_place(k):
            down = k // half
            return (1 - down) * (2 * k) + down * (2 * (n - k) - 1)

    right = at_place((place + 1) % n)
    left = at_place((place + n - 1) % n)
    pair = 1 - core

    barrier = pltpu.get_barrier_semaphore()
    for target in ({"vir": right}, {"vir": left}, {"occ": pair}):
        pl.semaphore_signal(barrier, inc=1, device_id=target, device_id_type=MESH)
    pl.semaphore_wait(barrier, 3)

    def own_part(slot, q):
        return buf.at[slot, pl.ds(0, occ_local), pl.ds(q * rows, rows)]

    def pair_part(slot, q):
        return buf.at[slot, pl.ds(occ_local, occ_local), pl.ds(q * rows, rows)]

    def to_right(slot, q, src=None):
        return pltpu.make_async_remote_copy(
            src_ref=own_part(slot, q) if src is None else src,
            dst_ref=own_part(slot + 1, q),
            send_sem=right_send.at[slot, q],
            recv_sem=right_recv.at[slot + 1, q],
            device_id={"vir": right},
            device_id_type=MESH,
        )

    def to_left(slot, q, src=None):
        return pltpu.make_async_remote_copy(
            src_ref=own_part(slot % n, q) if src is None else src,
            dst_ref=own_part(slot - 1, q),
            send_sem=left_send.at[n - slot, q],
            recv_sem=left_recv.at[n - slot + 1, q],
            device_id={"vir": left},
            device_id_type=MESH,
        )

    def to_pair(slot, q, src=None):
        return pltpu.make_async_remote_copy(
            src_ref=own_part(slot, q) if src is None else src,
            dst_ref=pair_part(slot, q),
            send_sem=pair_send.at[slot, q],
            recv_sem=pair_recv.at[slot, q],
            device_id={"occ": pair},
            device_id_type=MESH,
        )

    def x_part(q):
        return x_ref.at[:, pl.ds(q * rows, rows)]

    own_copy = pltpu.make_async_copy(x_ref, buf.at[0, pl.ds(0, occ_local)], local_sem)
    for q in range(chunks):
        to_right(0, q, x_part(q)).start()
        to_left(n, chunks - 1 - q, x_part(chunks - 1 - q)).start()
    own_copy.start()
    for q in range(chunks):
        to_pair(0, q, x_part(q)).start()
    out_ref[...] = jnp.zeros_like(out_ref)
    own_copy.wait()

    diagonal = lax.broadcasted_iota(jnp.int32, (vir_local, vir_local), 0) == (
        lax.broadcasted_iota(jnp.int32, (vir_local, vir_local), 1)
    )
    own_row = vir_ref[pl.ds(me, 1), :].astype(jnp.float32)
    own_column = jnp.sum(jnp.where(diagonal, own_row, 0.0), axis=1, keepdims=True)
    own_occ = [occ_ref[core * occ_local + i].astype(jnp.float32) for i in range(occ_local)]
    pair_occ = [occ_ref[pair * occ_local + i].astype(jnp.float32) for i in range(occ_local)]

    def compute(slot):
        source = at_place((place - slot + n) % n)
        energy_row = vir_ref[pl.ds(source, 1), :].astype(jnp.float32)
        base = own_column + energy_row
        amplitude = pair_amplitude(
            buf, 0, slot, base, own_occ, pair_occ, occ_local, vir_local, aux
        )

        step = 1024 if aux % 1024 == 0 else aux

        @pl.loop(0, aux // step)
        def _(t):
            columns = pl.ds(pl.multiple_of(t * step, step), step)
            there = buf[slot, :, :, columns].reshape(2 * occ_local * vir_local, step)
            part = jnp.dot(amplitude, there, preferred_element_type=jnp.float32)
            out_ref[:, :, columns] += part.reshape(occ_local, vir_local, step)

    def step_body(h, carry):
        @pl.when(h == 0)
        def _():
            for q in range(chunks):
                to_pair(0, q).wait_recv()

        @pl.when((h > 0) & (h < half))
        def _():
            for q in range(chunks):
                back = chunks - 1 - q
                to_right(h - 1, q).wait_recv()
                if q < chunks // 2:
                    to_right(h, q).start()
                else:
                    @pl.when(h < half - 1)
                    def _():
                        to_right(h, q).start()
                to_pair(h, q).start()
                to_left(n - h + 1, back).wait_recv()
                if back >= chunks // 2:
                    to_left(n - h, back).start()
                else:
                    @pl.when(h < half - 1)
                    def _():
                        to_left(n - h, back).start()
                to_pair(n - h, back).start()
            for q in range(chunks):
                to_pair(h, q).wait_recv()
                to_pair(n - h, chunks - 1 - q).wait_recv()

        @pl.when(h == half)
        def _():
            for q in range(chunks // 2):
                back = chunks - 1 - q
                to_right(half - 1, q).wait_recv()
                to_pair(half, q).start()
                to_left(half + 1, back).wait_recv()
                to_pair(half, back).start()
            for q in range(chunks):
                to_pair(half, q).wait_recv()

        both = jnp.where((h > 0) & (h < half), 2, 1)

        @pl.loop(0, both)
        def _(side):
            compute(h * (1 - side) + (n - h) * side)

        return carry

    lax.fori_loop(0, half + 1, step_body, 0)

    for h in range(half):
        for q in range(chunks):
            if h < half - 1 or q < chunks // 2:
                to_right(h, q).wait_send()
            if h < half - 1 or q >= chunks // 2:
                to_left(n - h, q, x_part(q) if h == 0 else None).wait_send()
    for slot in range(n):
        for q in range(chunks):
            to_pair(slot, q).wait_send()


def solution(mesh):
    n = mesh.shape["vir"]
    natural = ring_is_natural(mesh)
    grid = grid_of(mesh)

    def on_device(factors, occ_energy, vir_energy):
        occ_local, vir_local, aux = factors.shape
        dma = pltpu.SemaphoreType.DMA
        blocks = pltpu.VMEM((n, 2 * occ_local, vir_local, aux), jnp.bfloat16)
        parts, tiles = 8, 12
        fits = occ_local == 2 and vir_local == 128 and aux % (tiles * 128) == 0
        if grid and fits:
            chunks, wide = occ_local * parts, occ_local * vir_local
            early, lead = (4, 5), 3
            body = functools.partial(grid_kernel, chunks // 2, early, lead)
            scratch = [
                blocks,
                pltpu.VMEM((occ_local, vir_local, aux), jnp.float32),
                pltpu.VMEM((tiles, occ_local, vir_local, aux // tiles), jnp.bfloat16),
                pltpu.VMEM((tiles, occ_local, vir_local, aux // tiles), jnp.bfloat16),
                pltpu.VMEM((wide, 2 * wide), jnp.bfloat16),
                pltpu.VMEM((2, 2, wide, wide), jnp.bfloat16),
                dma,
                *[dma((3, chunks))] * 2,
                *[dma((2, chunks))] * 2,
                *[dma((3, chunks))] * 2,
                *[dma((n, parts))] * 2,
                *[dma((tiles,))] * 2,
                *[dma((2, 2))] * 2,
            ]
        else:
            chunks = 4
            body = functools.partial(kernel, n, natural, chunks)
            scratch = [
                blocks,
                dma,
                *[dma((n // 2, chunks)), dma((n // 2 + 1, chunks))] * 2,
                *[dma((n, chunks))] * 2,
            ]
        return pl.pallas_call(
            body,
            out_shape=pltpu.VMEM((occ_local, vir_local, aux), jnp.float32),
            in_specs=[
                pl.BlockSpec(memory_space=pl.ANY),
                pl.BlockSpec(memory_space=pltpu.SMEM),
                pl.BlockSpec(memory_space=pltpu.VMEM),
            ],
            out_specs=pl.BlockSpec(memory_space=pltpu.VMEM),
            scratch_shapes=scratch,
            compiler_params=pltpu.CompilerParams(
                collective_id=0, has_side_effects=True, vmem_limit_bytes=56 * 1024 * 1024
            ),
            name="ring_density",
        )(pltpu.with_memory_space_constraint(factors, pltpu.HBM), occ_energy, vir_energy.reshape(n, vir_local))

    return jax.shard_map(
        on_device,
        mesh=mesh,
        in_specs=(P(("frag", "occ"), "vir", None), P("frag"), P("frag")),
        out_specs=P(("frag", "occ"), "vir", None),
        check_vma=False,
    )
```
